32 devices in a mesh: groups: 2 (over y), tm: 8 (over z, core), chan: 2 (over x), rows: 1.
Axes of the slice: x: 2, y: 2, z: 4, core: 2. Of those that a mesh axis runs over, the one named last changes fastest.
Arguments:
- video: bfloat16 [32, 8, 32, 512], P(('groups', 'tm'), 'rows', None, 'chan'), parts along dimension 0, may hold values from -6 to 6
- channel_gain: float32 [512], P('chan'), may hold values from 0.1 to 1.9
- weights: bfloat16 [27, 512, 512], P(None, None, 'chan'), may hold values from -0.0546875 to 0.0546875
- lengths: int32 [8], P('groups'), parts along dimension 0, may hold values from 1 to 8, 16 in all
- cotangent: bfloat16 [32, 8, 32, 512], P(('groups', 'tm'), 'rows', None, 'chan'), parts along dimension 0, may hold values from -6 to 6
Outputs:
- output: bfloat16 [32, 8, 32, 512], P(('groups', 'tm'), 'rows', None, 'chan'), parts along dimension 0
- input_grad: bfloat16 [32, 8, 32, 512], P(('groups', 'tm'), 'rows', None, 'chan'), parts along dimension 0
- weight_grad: float32 [54, 512, 512], P('groups', ('tm', 'rows'), 'chan'), parts along dimension 0
The draws below stay inside these ranges and needn't reach their ends.
There are 2 independent parts, one for each index of `groups`. The reference program is written for one: setup_inputs(seed, part) draws one part's arguments, and reference() takes and returns one part's arrays. A program takes and returns all parts, laid end to end along the dimension named above; an argument that names none is the same for every part. Nothing has to cross between parts.
Inputs may be any that keep to these rules, and one draw needn't show every extreme that they name: The 4 lengths sum to 16; the longest is exactly 8.
All inputs are finite; a program needn't handle non-finite values.
Results may differ from the reference program's by a relative error of at most 0.004.
Values may be sent and summed in bfloat16 or wider, within the bound.
No kernel may reach another device: no remote copies, remote signals or barrier semaphores. Data moves between devices by JAX's collectives and lax.ppermute only.
A program may use at most 128 MiB of HBM per device.

```python
import math
import jax
import jax.numpy as jnp
import numpy as np
from jax import lax

C = 512
WID = 32
FRAMES = 16
HEIGHT = 8
CLIPS = 4
MOST = 8


def level_of(rng, dims, split, least, largest):
    factor_of, own = 1.0, jax.random.fold_in(rng, 6)
    for axis_at, blocks in split:
        draws = jnp.exp(jax.random.uniform(jax.random.fold_in(own, axis_at), (blocks,), jnp.float32, least / len(split), largest / len(split)))
        factor_of = factor_of * jnp.repeat(draws, dims[axis_at] // blocks).reshape([-1 if axis == axis_at else 1 for axis in range(len(dims))])
    return factor_of


def profile(count, total, most, slope):
    portions = [(1 << 20) // math.isqrt(rank ** slope) + 1 for rank in range(2, count + 1)]
    spare, counts = total - most - (count - 1), [1] * (count - 1)
    while spare > 0:
        candidates = [i for i in range(count - 1) if counts[i] < most]
        pool, budget = sum([portions[i] for i in candidates]), spare
        for i in candidates:
            addition = min(most - counts[i], max(1, budget * portions[i] // pool), spare)
            counts[i] = counts[i] + addition
            spare = spare - addition
    return np.array([most] + counts)


def ragged_sizes(own_key, amount, total, reach, slope):
    if amount == 2:
        one = jax.random.randint(own_key, (), max(1, total - reach), min(reach, total - 1) + 1)
        return jnp.stack([one, total - one])
    sizes = jnp.asarray(profile(amount, total, reach, slope), jnp.int32)
    twos = (amount - 1) // 2
    donor, sink = sizes[1:1 + 2 * twos:2], sizes[2:2 + 2 * twos:2]
    room = jnp.minimum(donor - 1, reach - sink)
    passed = jax.random.randint(jax.random.fold_in(own_key, 1), (twos,), 0, 1 << 20) % (room + 1)
    sizes = sizes.at[1:1 + 2 * twos:2].set(donor - passed).at[2:2 + 2 * twos:2].set(sink + passed)
    return sizes[jax.random.permutation(jax.random.fold_in(own_key, 2), amount)]


def scatter_about(key, shape, width, reach, shards=(), kind=jnp.bfloat16):
    gain = level_of(key, shape, shards, -0.22, 0.18) if shards else 1.0
    drawn = jax.random.normal(key, shape, jnp.float32) * width * gain
    return jnp.minimum(jnp.maximum(drawn, -reach), reach).astype(kind)


def setup_inputs(seed: int = 0, part: int = 0) -> dict:
    keys = jax.random.split(jax.random.key(seed), 6)
    own_keys = jax.random.split(jax.random.fold_in(keys[5], part), 6)
    return {
        "video": scatter_about(own_keys[0], (FRAMES, HEIGHT, WID, C), 1.0, 6.0, ((0, 8), (3, 2))),
        "channel_gain": jnp.clip(1.0 + 0.18 * jax.random.normal(keys[1], (C,), jnp.float32), 0.1, 1.9),
        "weights": scatter_about(keys[2], (27, C, C), (27 * C) ** -0.5, 0.0546875, ((2, 2),)),
        "lengths": ragged_sizes(own_keys[3], CLIPS, FRAMES, MOST, 0).astype(jnp.int32),
        "cotangent": scatter_about(own_keys[4], (FRAMES, HEIGHT, WID, C), 1.0, 6.0, ((0, 8), (3, 2))),
    }


def clip_tables(lengths, frame_ids):
    clip_lens = lengths.astype(jnp.int32)
    clip_ends = jnp.cumsum(clip_lens).astype(jnp.int32)
    clip_starts = (clip_ends - clip_lens).astype(jnp.int32)
    clip_ids = lax.optimization_barrier(jnp.sum((frame_ids[:, None] >= clip_ends[None, :]).astype(jnp.int32), axis=1)).astype(jnp.int32)
    clip_first = lax.optimization_barrier(jnp.max(jnp.where(clip_starts[None, :] <= frame_ids[:, None], clip_starts[None, :], 0), axis=1)).astype(jnp.int32)
    opening = jnp.any(clip_starts[None, :] == frame_ids[:, None], axis=1)
    return (clip_ids, clip_first, opening)

def reference(video, channel_gain, weights, lengths, cotangent):
    frame_count, row_count, col_count, all_chans = video.shape
    pixel_count = frame_count * row_count * col_count
    frame_ids = jnp.arange(frame_count + 2, dtype=jnp.int32)
    clip_ids, clip_first, opening = clip_tables(lengths, frame_ids)
    own_frames = frame_ids[:frame_count]
    scaled = video.astype(jnp.float32) * channel_gain
    activated = jax.nn.silu(scaled).astype(jnp.bfloat16)
    act_pad = jnp.pad(activated, ((0, 0), (1, 1), (1, 1), (0, 0)))
    grad_pad = jnp.pad(cotangent, ((0, 0), (1, 1), (1, 1), (0, 0)))
    flat_grad = cotangent.reshape(pixel_count, all_chans)
    output_sum = jnp.zeros((pixel_count, all_chans), jnp.float32)
    weight_terms = []
    lagged = []
    for lag_step in range(3):
        source = jnp.maximum(own_frames - lag_step, clip_first[:frame_count]).astype(jnp.int32)
        chosen = jnp.take(act_pad, source, axis=0)
        tap_stack = jnp.stack([chosen[:, row_step:row_step + row_count, col_step:col_step + col_count, :] for row_step in range(3) for col_step in range(3)], axis=3).reshape(pixel_count, 9 * all_chans)
        kernel = weights[9 * lag_step:9 * lag_step + 9].reshape(9 * all_chans, all_chans)
        output_sum = output_sum + jnp.dot(tap_stack, kernel, preferred_element_type=jnp.float32)
        weight_terms.append(lax.dot_general(tap_stack, flat_grad, (((0,), (0,)), ((), ())), preferred_element_type=jnp.float32).reshape(9, all_chans, all_chans))
        back_stack = jnp.stack([grad_pad[:, 2 - row_step:2 - row_step + row_count, 2 - col_step:2 - col_step + col_count, :] for row_step in range(3) for col_step in range(3)], axis=3).reshape(pixel_count, 9 * all_chans)
        back_kernel = jnp.transpose(weights[9 * lag_step:9 * lag_step + 9], (0, 2, 1)).reshape(9 * all_chans, all_chans)
        partial_value = jnp.dot(back_stack, back_kernel, preferred_element_type=jnp.float32).reshape(frame_count, row_count, col_count, all_chans)
        lagged.append(jnp.pad(partial_value, ((0, 2), (0, 0), (0, 0), (0, 0))))
    here_ids = clip_ids[:frame_count]
    start_flag = opening[:frame_count].astype(jnp.float32)
    act_grad = jnp.zeros((frame_count, row_count, col_count, all_chans), jnp.float32)
    for lag_step in range(3):
        same_clip = (clip_ids[lag_step:lag_step + frame_count] == here_ids).astype(jnp.float32)
        act_grad = act_grad + same_clip[:, None, None, None] * lagged[lag_step][lag_step:lag_step + frame_count]
        for inner_step in range(lag_step):
            near_clip = (clip_ids[inner_step:inner_step + frame_count] == here_ids).astype(jnp.float32) * start_flag
            act_grad = act_grad + near_clip[:, None, None, None] * lagged[lag_step][inner_step:inner_step + frame_count]
    output = (video.astype(jnp.float32) + output_sum.reshape(frame_count, row_count, col_count, all_chans)).astype(jnp.bfloat16)
    sigmoid_value = jax.nn.sigmoid(scaled)
    slope_factor = sigmoid_value * (1.0 + scaled * (1.0 - sigmoid_value))
    input_grad = (cotangent.astype(jnp.float32) + act_grad * slope_factor * channel_gain).astype(jnp.bfloat16)
    weight_grad = jnp.concatenate(weight_terms, axis=0) * (1.0 / math.sqrt(pixel_count))
    return (output, input_grad, weight_grad)
```

```python
import functools, math
import jax, jax.numpy as jnp
from jax import lax
from jax.experimental import pallas as pl
from jax.experimental.pallas import tpu as pltpu
from jax.sharding import PartitionSpec as P


LAGS = 3
SIDE = 3


def first_of(lens, count, frame):
    start, first = jnp.int32(0), jnp.int32(0)
    for i in range(count):
        first = jnp.where(start <= frame, start, first)
        start = start + lens[i]
    return first


def opens(lens, count, frame):
    start, hit = jnp.int32(0), jnp.int32(0)
    for i in range(count):
        hit = jnp.where(start == frame, 1, hit)
        start = start + lens[i]
    return hit


def joined(lens, count, frame, later):
    end, cut = jnp.int32(0), jnp.int32(0)
    for i in range(count):
        end = end + lens[i]
        cut = jnp.where((frame < end) & (end <= later), 1, cut)
    return 1 - cut


def moved(value, steps, width):
    rows = value.shape[0]
    col = lax.broadcasted_iota(jnp.int32, value.shape, 0) % width
    if steps == 1:
        return jnp.where(col == width - 1, 0.0, pltpu.roll(value, rows - 1, 0))
    return jnp.where(col == 0, 0.0, pltpu.roll(value, 1, 0))


def forward_body(parts, clips, where_ref, lens, video, *refs):
    own, past = refs[:parts], refs[parts : 2 * parts]
    weights, out, padded, acc = refs[2 * parts :]
    frames, rows, width, chans = video.shape
    step = pl.program_id(0)
    base, chan = where_ref[0], where_ref[1]

    @pl.when(step == 0)
    def _():
        edge = jnp.zeros((2 * frames, 1, width, chans), padded.dtype)
        for j in range(parts):
            padded[j, :, 0:1] = edge
            padded[j, :, rows + 1 : rows + 2] = edge
            padded[j, 0:frames, 1 : rows + 1] = past[j][...]
            padded[j, frames : 2 * frames, 1 : rows + 1] = own[j][...]
        acc[...] = jnp.zeros_like(acc)

    lag, row_step = step // SIDE, step % SIDE
    for j in range(parts):
        shard = lax.rem(chan + j, parts)
        taps = []
        for f in range(frames):
            frame = base + f
            source = jnp.maximum(frame - lag, first_of(lens, clips, frame)) - base + frames
            taps.append(padded[j, source, pl.ds(row_step, rows)].reshape(rows * width, chans))
        taps = jnp.concatenate(taps, axis=0)
        for b in range(SIDE):
            kernel = weights[b, pl.ds(pl.multiple_of(shard * chans, chans), chans), :]
            acc[b] += jnp.dot(taps, kernel, preferred_element_type=jnp.float32)

    @pl.when(step == LAGS * SIDE - 1)
    def _():
        total = acc[1] + moved(acc[0], -1, width) + moved(acc[2], 1, width)
        out[...] = (video[...].astype(jnp.float32) + total.reshape(video.shape)).astype(out.dtype)


def forward(where, lens, video, own, past, weights):
    frames, rows, width, chans = video.shape
    parts, pixels = len(own), frames * rows * width
    whole = pl.BlockSpec(memory_space=pltpu.VMEM)
    smem = pl.BlockSpec(memory_space=pltpu.SMEM)
    flops = 2 * pixels * weights.shape[0] * weights.shape[1] * weights.shape[2]
    return pl.pallas_call(
        functools.partial(forward_body, parts, lens.shape[0]),
        grid=(LAGS * SIDE,),
        out_shape=jax.ShapeDtypeStruct(video.shape, video.dtype),
        in_specs=[smem, smem, whole] + [whole] * (2 * parts)
        + [pl.BlockSpec((SIDE,) + weights.shape[1:], lambda i: (i, 0, 0))],
        out_specs=whole,
        scratch_shapes=[
            pltpu.VMEM((parts, 2 * frames, rows + 2, width, chans), video.dtype),
            pltpu.VMEM((SIDE, pixels, weights.shape[2]), jnp.float32),
        ],
        compiler_params=pltpu.CompilerParams(vmem_limit_bytes=24 << 20),
        cost_estimate=pl.CostEstimate(flops=flops, transcendentals=0, bytes_accessed=2 * weights.size),
        name="forward",
    )(where, lens, video, *own, *past, weights)


def backward_body(parts, clips, where_ref, lens, own, later, weights, mine, *refs):
    others, (mixed, acc) = refs[: parts - 1], refs[parts - 1 :]
    frames, rows, width, chans = own.shape
    step = pl.program_id(0)
    base, chan = where_ref[0], where_ref[1]

    @pl.when(step == 0)
    def _():
        mixed[:, :, 0:1] = jnp.zeros((LAGS, frames, 1, width, chans), mixed.dtype)
        mixed[:, :, rows + 1 : rows + 2] = jnp.zeros((LAGS, frames, 1, width, chans), mixed.dtype)
        take = lambda f: (own[f] if f < frames else later[f - frames]).astype(jnp.float32)
        for f in range(frames):
            frame = base + f
            start = opens(lens, clips, frame).astype(jnp.float32)
            next_one = joined(lens, clips, frame, frame + 1).astype(jnp.float32)
            next_two = joined(lens, clips, frame, frame + 2).astype(jnp.float32)
            mixed[0, f, 1 : rows + 1] = own[f]
            mixed[1, f, 1 : rows + 1] = (next_one * take(f + 1) + start * take(f)).astype(mixed.dtype)
            mixed[2, f, 1 : rows + 1] = (
                next_two * take(f + 2) + start * (take(f) + next_one * take(f + 1))
            ).astype(mixed.dtype)
        acc[...] = jnp.zeros_like(acc)

    lag, row_step = step // SIDE, step % SIDE
    taps = mixed[lag, :, pl.ds(2 - row_step, rows)].reshape(frames * rows * width, chans)
    for j in range(parts):
        shard = lax.rem(chan + j, parts)
        for b in range(SIDE):
            kernel = weights[b, pl.ds(pl.multiple_of(shard * chans, chans), chans), :]
            acc[j, b] += lax.dot_general(
                taps, kernel, (((1,), (1,)), ((), ())), preferred_element_type=jnp.float32
            )

    @pl.when(step == LAGS * SIDE - 1)
    def _():
        for j in range(parts):
            total = acc[j, 1] + moved(acc[j, 0], 1, width) + moved(acc[j, 2], -1, width)
            if j == 0:
                mine[...] = total.reshape(mine.shape)
            else:
                others[j - 1][...] = total.reshape(mine.shape).astype(others[j - 1].dtype)


def backward(where, lens, own, later, weights):
    frames, rows, width, chans = own.shape
    parts, pixels = weights.shape[1] // chans, frames * rows * width
    whole = pl.BlockSpec(memory_space=pltpu.VMEM)
    smem = pl.BlockSpec(memory_space=pltpu.SMEM)
    flops = 2 * pixels * weights.shape[0] * weights.shape[1] * weights.shape[2]
    return pl.pallas_call(
        functools.partial(backward_body, parts, lens.shape[0]),
        grid=(LAGS * SIDE,),
        out_shape=[jax.ShapeDtypeStruct(own.shape, jnp.float32)]
        + [jax.ShapeDtypeStruct(own.shape, own.dtype)] * (parts - 1),
        in_specs=[smem, smem, whole, whole, pl.BlockSpec((SIDE,) + weights.shape[1:], lambda i: (i, 0, 0))],
        out_specs=[whole] * parts,
        scratch_shapes=[
            pltpu.VMEM((LAGS, frames, rows + 2, width, chans), own.dtype),
            pltpu.VMEM((parts, SIDE, pixels, chans), jnp.float32),
        ],
        compiler_params=pltpu.CompilerParams(vmem_limit_bytes=24 << 20),
        cost_estimate=pl.CostEstimate(flops=flops, transcendentals=0, bytes_accessed=2 * weights.size),
        name="backward",
    )(where, lens, own, later, weights)


def turned_body(parts, where_ref, *refs):
    own, out = refs[:parts], refs[parts]
    chans = own[0].shape[1]
    for j in range(parts):
        shard = lax.rem(where_ref[1] + j, parts)
        out[pl.ds(pl.multiple_of(shard * chans, chans), chans), :] = own[j][...].T


def turned(where, own):
    pixels, chans = own[0].shape
    whole = pl.BlockSpec(memory_space=pltpu.VMEM)
    return pl.pallas_call(
        functools.partial(turned_body, len(own)),
        out_shape=jax.ShapeDtypeStruct((len(own) * chans, pixels), own[0].dtype),
        in_specs=[pl.BlockSpec(memory_space=pltpu.SMEM)] + [whole] * len(own),
        out_specs=whole,
        cost_estimate=pl.CostEstimate(flops=pixels * chans * 64, transcendentals=0, bytes_accessed=4 * pixels * chans),
        name="turned",
    )(where, *own)


def weight_body(blocks, frames, rows, width, clips, scale, where_ref, lens, turned_ref, *refs):
    cots, (out, taps) = refs[:blocks], refs[blocks:]
    chans, pixels = turned_ref.shape[1:]
    area = rows * width
    shard = where_ref[2]

    place = lax.broadcasted_iota(jnp.int32, (1, pixels), 1)
    row, col = (place % area) // width, place % width
    masks = {}
    for a in range(SIDE):
        for b in range(SIDE):
            r, c = row + a - 1, col + b - 1
            masks[a, b] = ((r >= 0) & (r < rows) & (c >= 0) & (c < width)).astype(jnp.float32)

    def spread(block, carry):
        value = turned_ref[block].astype(jnp.float32)
        for a in range(SIDE):
            for b in range(SIDE):
                step = (a - 1) * width + b - 1
                copy = value if step == 0 else pltpu.roll(value, (-step) % pixels, 1) * masks[a, b]
                copy = copy.astype(taps.dtype)
                at = (SIDE * a + b) * chans
                for f in range(frames):
                    taps[block * frames + f, at : at + chans] = copy[:, f * area : (f + 1) * area]
        return carry

    lax.fori_loop(0, blocks, spread, 0)
    for offset in range(blocks):
        first = (shard ^ offset) * frames

        def lagged(lag, carry, offset=offset, first=first):
            pieces = []
            for f in range(frames):
                frame = first + f
                source = jnp.maximum(frame - lag, first_of(lens, clips, frame))
                pieces.append(taps[source])
            terms = jnp.dot(jnp.concatenate(pieces, axis=1), cots[offset][...], preferred_element_type=jnp.float32)
            at = pl.ds(lag * SIDE * SIDE, SIDE * SIDE)
            terms = terms.reshape(SIDE * SIDE, chans, terms.shape[1])
            if offset == 0:
                out[at] = terms
            elif offset == blocks - 1:
                out[at] = (out[at] + terms) * scale
            else:
                out[at] += terms
            return carry

        lax.fori_loop(0, LAGS, lagged, 0)


def weight_terms(where, lens, turned_blocks, cots, rows, width, scale):
    blocks, chans, pixels = turned_blocks.shape
    area = rows * width
    frames = pixels // area
    outs = cots[0].shape[1]
    whole = pl.BlockSpec(memory_space=pltpu.VMEM)
    smem = pl.BlockSpec(memory_space=pltpu.SMEM)
    taps = SIDE * SIDE
    return pl.pallas_call(
        functools.partial(weight_body, blocks, frames, rows, width, lens.shape[0], scale),
        out_shape=jax.ShapeDtypeStruct((LAGS * taps, chans, outs), jnp.float32),
        in_specs=[smem, smem, whole] + [whole] * blocks,
        out_specs=whole,
        scratch_shapes=[pltpu.VMEM((blocks * frames, taps * chans, area), turned_blocks.dtype)],
        compiler_params=pltpu.CompilerParams(vmem_limit_bytes=28 << 20),
        cost_estimate=pl.CostEstimate(
            flops=2 * blocks * pixels * LAGS * taps * chans * outs, transcendentals=0, bytes_accessed=8 << 20),
        name="weight_terms",
    )(where, lens, turned_blocks, *cots)


def extended_2(cells, sides, width):
    for axis, dim in sides:
        count = lax.axis_size(axis)
        ends = count - 1
        head = lax.slice_in_dim(cells, 0, width, axis=dim)
        tail = lax.slice_in_dim(cells, cells.shape[dim] - width, cells.shape[dim], axis=dim)
        cells = jnp.concatenate(
            [
                lax.ppermute(tail, axis, [(i, (i + 1) % count) for i in range(ends)]),
                cells,
                lax.ppermute(head, axis, [((i + 1) % count, i) for i in range(ends)]),
            ],
            axis=dim,
        )
    return cells


def shifted(value, axis, steps):
    count = lax.axis_size(axis)
    leading, last = (max(0, -steps), min(count, count - steps))
    return lax.ppermute(value, axis, [(source, source + steps) for source in range(leading, last)])


def clip_tables(lengths, frame_ids):
    clip_ends = jnp.cumsum(lengths)
    clip_starts = clip_ends - lengths
    clip_ids = jnp.sum((frame_ids[:, None] >= clip_ends[None, :]).astype(jnp.int32), axis=1)
    clip_first = jnp.max(
        jnp.where(clip_starts[None, :] <= frame_ids[:, None], clip_starts[None, :], 0), axis=1
    )
    opening = jnp.any(clip_starts[None, :] == frame_ids[:, None], axis=1)
    return (clip_ids, clip_first, opening)


def input_terms(grad_frames, weights, row_count, col_count):
    frame_total = grad_frames.shape[0]
    local_chans = grad_frames.shape[3]
    all_chans = weights.shape[1]
    pieces = []
    for lag_step in range(3):
        back_stack = jnp.stack(
            [
                grad_frames[
                    :,
                    2 - row_step : 2 - row_step + row_count,
                    2 - col_step : 2 - col_step + col_count,
                    :,
                ]
                for row_step in range(3)
                for col_step in range(3)
            ],
            axis=3,
        ).reshape(frame_total * row_count * col_count, 9 * local_chans)
        back_kernel = jnp.transpose(weights[9 * lag_step : 9 * lag_step + 9], (0, 2, 1)).reshape(
            9 * local_chans, all_chans
        )
        pieces.append(
            jnp.dot(back_stack, back_kernel, preferred_element_type=jnp.float32).reshape(
                frame_total, row_count, col_count, all_chans
            )
        )
    return pieces


def lag_mix(lagged, clip_ids, opening, frame_count):
    here_ids = clip_ids[:frame_count]
    start_flag = opening[:frame_count].astype(jnp.float32)
    act_grad = jnp.zeros((frame_count,) + lagged[0].shape[1:], jnp.float32)
    for lag_step in range(3):
        same_clip = (clip_ids[lag_step : lag_step + frame_count] == here_ids).astype(jnp.float32)
        act_grad = (
            act_grad
            + same_clip[:, None, None, None] * lagged[lag_step][lag_step : lag_step + frame_count]
        )
        for inner_step in range(lag_step):
            near_clip = (clip_ids[inner_step : inner_step + frame_count] == here_ids).astype(
                jnp.float32
            ) * start_flag
            act_grad = (
                act_grad
                + near_clip[:, None, None, None]
                * lagged[lag_step][inner_step : inner_step + frame_count]
            )
    return act_grad


def split_rows(video, channel_gain, weights, lengths, cotangent):
    frame_count, row_count, col_count, local_chans = video.shape
    all_chans = weights.shape[1]
    pixel_count = frame_count * row_count * col_count
    total_pixels = pixel_count * lax.axis_size("tm") * lax.axis_size("rows")
    frame_base = lax.axis_index("tm") * frame_count
    frame_ids = frame_base + jnp.arange(frame_count + 2, dtype=jnp.int32)
    clip_ids, clip_first, opening = clip_tables(lengths, frame_ids)
    own_frames = frame_ids[:frame_count]
    scaled = video.astype(jnp.float32) * channel_gain
    activated = jax.nn.silu(scaled).astype(jnp.bfloat16)
    paired = extended_2(jnp.stack([activated, cotangent]), (("rows", 2),), 1)
    paired = jnp.pad(paired, ((0, 0), (0, 0), (0, 0), (1, 1), (0, 0)))
    act_pad = paired[0]
    grad_pad = paired[1]
    prior_rows = shifted(act_pad, "tm", 1)
    extended = jnp.concatenate([prior_rows, act_pad], axis=0)
    gathered = lax.all_gather(extended, "chan", axis=3, tiled=True)
    flat_grad = cotangent.reshape(pixel_count, local_chans)
    output_sum = jnp.zeros((pixel_count, local_chans), jnp.float32)
    weight_terms = []
    for lag_step in range(3):
        distance = jnp.minimum(lag_step, own_frames - clip_first[:frame_count])[:, None, None, None]
        chosen = jnp.where(
            distance == 0,
            gathered[2 : frame_count + 2],
            jnp.where(distance == 1, gathered[1 : frame_count + 1], gathered[0:frame_count]),
        )
        tap_stack = jnp.stack(
            [
                chosen[:, row_step : row_step + row_count, col_step : col_step + col_count, :]
                for row_step in range(3)
                for col_step in range(3)
            ],
            axis=3,
        ).reshape(pixel_count, 9 * all_chans)
        kernel = weights[9 * lag_step : 9 * lag_step + 9].reshape(9 * all_chans, local_chans)
        output_sum = output_sum + jnp.dot(tap_stack, kernel, preferred_element_type=jnp.float32)
        weight_terms.append(
            lax.dot_general(
                tap_stack, flat_grad, (((0,), (0,)), ((), ())), preferred_element_type=jnp.float32
            ).reshape(9, all_chans, local_chans)
        )
    output = (
        video.astype(jnp.float32)
        + output_sum.reshape(frame_count, row_count, col_count, local_chans)
    ).astype(jnp.bfloat16)
    own_terms = lax.psum_scatter(
        jnp.stack(input_terms(grad_pad, weights, row_count, col_count)),
        "chan",
        scatter_dimension=4,
        tiled=True,
    )
    arriving = shifted(
        jnp.concatenate([own_terms[1, 0:1], own_terms[2, 0:2]], axis=0).astype(jnp.bfloat16),
        "tm",
        -1,
    ).astype(jnp.float32)
    lagged = [
        own_terms[0],
        jnp.concatenate([own_terms[1], arriving[0:1]], axis=0),
        jnp.concatenate([own_terms[2], arriving[1:3]], axis=0),
    ]
    act_grad = lag_mix(lagged, clip_ids, opening, frame_count)
    sigmoid_value = jax.nn.sigmoid(scaled)
    slope_factor = sigmoid_value * (1.0 + scaled * (1.0 - sigmoid_value))
    input_grad = (cotangent.astype(jnp.float32) + act_grad * slope_factor * channel_gain).astype(
        jnp.bfloat16
    )
    weight_sum = jnp.concatenate(weight_terms, axis=0)
    summed = lax.psum_scatter(weight_sum, ("tm", "rows"), scatter_dimension=1, tiled=True)
    weight_grad = summed * (1.0 / math.sqrt(total_pixels))
    return (output, input_grad, weight_grad)


def along(value, axis, steps):
    count = lax.axis_size(axis)
    first, last = max(0, -steps), min(count, count - steps)
    return lax.ppermute(value, axis, [(source, source + steps) for source in range(first, last)])


def across(value, axis, offset):
    return lax.ppermute(value, axis, [(i, i ^ offset) for i in range(lax.axis_size(axis))])


def ahead(value, axis, steps):
    count = lax.axis_size(axis)
    return lax.ppermute(value, axis, [((i + steps) % count, i) for i in range(count)])


def gathered_blocks(own, axis):
    blocks = {0: own}
    bit = lax.axis_size(axis) // 2
    while bit:
        for offset in list(blocks):
            blocks[offset ^ bit] = across(blocks[offset], axis, bit)
        bit //= 2
    return [blocks[offset] for offset in range(len(blocks))]


def whole_rows(video, channel_gain, weights, lengths, cotangent):
    frames, rows, width, chans = video.shape
    all_chans = weights.shape[1]
    parts, shards = all_chans // chans, lax.axis_size("tm")
    pixels = frames * rows * width
    shard, chan = lax.axis_index("tm"), lax.axis_index("chan")
    where = jnp.stack([shard * frames, chan, shard]).astype(jnp.int32)
    scaled = video.astype(jnp.float32) * channel_gain
    activated = jax.nn.silu(scaled).astype(jnp.bfloat16)
    own = [activated] + [ahead(activated, "chan", j) for j in range(1, parts)]
    before = along(activated, "tm", 1)
    past = [before] + [ahead(before, "chan", j) for j in range(1, parts)]
    later = along(cotangent, "tm", -1)
    cots = gathered_blocks(cotangent.reshape(pixels, chans), "tm")
    mine, *others = backward(where, lengths, cotangent, later, weights)
    act_grad = mine
    for j in range(1, parts):
        act_grad = act_grad + ahead(others[j - 1], "chan", parts - j).astype(jnp.float32)
    blocks = turned(where, [x.reshape(pixels, chans) for x in own])
    blocks = lax.all_to_all(blocks.reshape(shards, all_chans // shards, pixels), "tm", 0, 0)
    output = forward(where, lengths, video, own, past, weights)
    sigmoid_value = jax.nn.sigmoid(scaled)
    slope_factor = sigmoid_value * (1.0 + scaled * (1.0 - sigmoid_value))
    input_grad = (cotangent.astype(jnp.float32) + act_grad * slope_factor * channel_gain).astype(jnp.bfloat16)
    scale = 1.0 / math.sqrt(pixels * shards)
    weight_grad = weight_terms(where, lengths, blocks, cots, rows, width, scale)
    return (output, input_grad, weight_grad)


def solution(mesh):
    in_specs = (
        P(("groups", "tm"), "rows", None, "chan"),
        P("chan"),
        P(None, None, "chan"),
        P("groups"),
        P(("groups", "tm"), "rows", None, "chan"),
    )
    out_specs = (
        P(("groups", "tm"), "rows", None, "chan"),
        P(("groups", "tm"), "rows", None, "chan"),
        P("groups", ("tm", "rows"), "chan"),
    )
    body = whole_rows if mesh.shape["rows"] == 1 else split_rows
    return jax.shard_map(body, mesh=mesh, in_specs=in_specs, out_specs=out_specs, check_vma=False)
```

```python
import functools, math
import jax, jax.numpy as jnp
from jax import lax
from jax.experimental import pallas as pl
from jax.experimental.pallas import tpu as pltpu
from jax.sharding import PartitionSpec as P


LAGS = 3
SIDE = 3


def first_of(lens, count, frame):
    start, first = jnp.int32(0), jnp.int32(0)
    for i in range(count):
        first = jnp.where(start <= frame, start, first)
        start = start + lens[i]
    return first


def opens(lens, count, frame):
    start, hit = jnp.int32(0), jnp.int32(0)
    for i in range(count):
        hit = jnp.where(start == frame, 1, hit)
        start = start + lens[i]
    return hit


def joined(lens, count, frame, later):
    end, cut = jnp.int32(0), jnp.int32(0)
    for i in range(count):
        end = end + lens[i]
        cut = jnp.where((frame < end) & (end <= later), 1, cut)
    return 1 - cut


def moved(value, steps, width):
    rows = value.shape[0]
    col = lax.broadcasted_iota(jnp.int32, value.shape, 0) % width
    if steps == 1:
        return jnp.where(col == width - 1, 0.0, pltpu.roll(value, rows - 1, 0))
    return jnp.where(col == 0, 0.0, pltpu.roll(value, 1, 0))


def silu_body(video, gain, out):
    scaled = video[...].astype(jnp.float32) * gain[...]
    out[...] = (scaled / (1.0 + jnp.exp(-scaled))).astype(out.dtype)


def silu(video, gain):
    whole = pl.BlockSpec(memory_space=pltpu.VMEM)
    return pl.pallas_call(
        silu_body,
        out_shape=jax.ShapeDtypeStruct(video.shape, video.dtype),
        in_specs=[whole, whole],
        out_specs=whole,
        cost_estimate=pl.CostEstimate(flops=8 * video.size, transcendentals=video.size, bytes_accessed=4 * video.size),
        name="silu",
    )(video, gain.reshape(1, -1))


def forward_body(parts, clips, where_ref, lens, video, *refs):
    own, past = refs[:parts], refs[parts : 2 * parts]
    weights, out, padded, acc = refs[2 * parts :]
    frames, rows, width, chans = video.shape
    step = pl.program_id(0)
    base, chan = where_ref[0], where_ref[1]

    @pl.when(step == 0)
    def _():
        edge = jnp.zeros((2 * frames, 1, width, chans), padded.dtype)
        for j in range(parts):
            padded[j, :, 0:1] = edge
            padded[j, :, rows + 1 : rows + 2] = edge
            padded[j, 0:frames, 1 : rows + 1] = past[j][...]
            padded[j, frames : 2 * frames, 1 : rows + 1] = own[j][...]
        acc[...] = jnp.zeros_like(acc)

    lag, row_step = step // SIDE, step % SIDE
    for j in range(parts):
        shard = lax.rem(chan + j, parts)
        taps = []
        for f in range(frames):
            frame = base + f
            source = jnp.maximum(frame - lag, first_of(lens, clips, frame)) - base + frames
            taps.append(padded[j, source, pl.ds(row_step, rows)].reshape(rows * width, chans))
        taps = jnp.concatenate(taps, axis=0)
        for b in range(SIDE):
            kernel = weights[b, pl.ds(pl.multiple_of(shard * chans, chans), chans), :]
            acc[b] += jnp.dot(taps, kernel, preferred_element_type=jnp.float32)

    @pl.when(step == LAGS * SIDE - 1)
    def _():
        total = acc[1] + moved(acc[0], -1, width) + moved(acc[2], 1, width)
        out[...] = (video[...].astype(jnp.float32) + total.reshape(video.shape)).astype(out.dtype)


def forward(where, lens, video, own, past, weights):
    frames, rows, width, chans = video.shape
    parts, pixels = len(own), frames * rows * width
    whole = pl.BlockSpec(memory_space=pltpu.VMEM)
    smem = pl.BlockSpec(memory_space=pltpu.SMEM)
    flops = 2 * pixels * weights.shape[0] * weights.shape[1] * weights.shape[2]
    return pl.pallas_call(
        functools.partial(forward_body, parts, lens.shape[0]),
        grid=(LAGS * SIDE,),
        out_shape=jax.ShapeDtypeStruct(video.shape, video.dtype),
        in_specs=[smem, smem, whole] + [whole] * (2 * parts)
        + [pl.BlockSpec((SIDE,) + weights.shape[1:], lambda i: (i, 0, 0))],
        out_specs=whole,
        scratch_shapes=[
            pltpu.VMEM((parts, 2 * frames, rows + 2, width, chans), video.dtype),
            pltpu.VMEM((SIDE, pixels, weights.shape[2]), jnp.float32),
        ],
        compiler_params=pltpu.CompilerParams(vmem_limit_bytes=24 << 20),
        cost_estimate=pl.CostEstimate(flops=flops, transcendentals=0, bytes_accessed=2 * weights.size),
        name="forward",
    )(where, lens, video, *own, *past, weights)


def backward_body(parts, clips, where_ref, lens, own, later, weights, mine, *refs):
    others, (mixed, acc) = refs[: parts - 1], refs[parts - 1 :]
    frames, rows, width, chans = own.shape
    step = pl.program_id(0)
    base, chan = where_ref[0], where_ref[1]

    @pl.when(step == 0)
    def _():
        mixed[:, :, 0:1] = jnp.zeros((LAGS, frames, 1, width, chans), mixed.dtype)
        mixed[:, :, rows + 1 : rows + 2] = jnp.zeros((LAGS, frames, 1, width, chans), mixed.dtype)
        take = lambda f: (own[f] if f < frames else later[f - frames]).astype(jnp.float32)
        for f in range(frames):
            frame = base + f
            start = opens(lens, clips, frame).astype(jnp.float32)
            next_one = joined(lens, clips, frame, frame + 1).astype(jnp.float32)
            next_two = joined(lens, clips, frame, frame + 2).astype(jnp.float32)
            mixed[0, f, 1 : rows + 1] = own[f]
            mixed[1, f, 1 : rows + 1] = (next_one * take(f + 1) + start * take(f)).astype(mixed.dtype)
            mixed[2, f, 1 : rows + 1] = (
                next_two * take(f + 2) + start * (take(f) + next_one * take(f + 1))
            ).astype(mixed.dtype)
        acc[...] = jnp.zeros_like(acc)

    lag, row_step = step // SIDE, step % SIDE
    taps = mixed[lag, :, pl.ds(2 - row_step, rows)].reshape(frames * rows * width, chans)
    for j in range(parts):
        shard = lax.rem(chan + j, parts)
        for b in range(SIDE):
            kernel = weights[b, pl.ds(pl.multiple_of(shard * chans, chans), chans), :]
            acc[j, b] += lax.dot_general(
                taps, kernel, (((1,), (1,)), ((), ())), preferred_element_type=jnp.float32
            )

    @pl.when(step == LAGS * SIDE - 1)
    def _():
        for j in range(parts):
            total = acc[j, 1] + moved(acc[j, 0], 1, width) + moved(acc[j, 2], -1, width)
            if j == 0:
                mine[...] = total.reshape(mine.shape)
            else:
                others[j - 1][...] = total.reshape(mine.shape).astype(others[j - 1].dtype)


def backward(where, lens, own, later, weights):
    frames, rows, width, chans = own.shape
    parts, pixels = weights.shape[1] // chans, frames * rows * width
    whole = pl.BlockSpec(memory_space=pltpu.VMEM)
    smem = pl.BlockSpec(memory_space=pltpu.SMEM)
    flops = 2 * pixels * weights.shape[0] * weights.shape[1] * weights.shape[2]
    return pl.pallas_call(
        functools.partial(backward_body, parts, lens.shape[0]),
        grid=(LAGS * SIDE,),
        out_shape=[jax.ShapeDtypeStruct(own.shape, jnp.float32)]
        + [jax.ShapeDtypeStruct(own.shape, own.dtype)] * (parts - 1),
        in_specs=[smem, smem, whole, whole, pl.BlockSpec((SIDE,) + weights.shape[1:], lambda i: (i, 0, 0))],
        out_specs=[whole] * parts,
        scratch_shapes=[
            pltpu.VMEM((LAGS, frames, rows + 2, width, chans), own.dtype),
            pltpu.VMEM((parts, SIDE, pixels, chans), jnp.float32),
        ],
        compiler_params=pltpu.CompilerParams(vmem_limit_bytes=24 << 20),
        cost_estimate=pl.CostEstimate(flops=flops, transcendentals=0, bytes_accessed=2 * weights.size),
        name="backward",
    )(where, lens, own, later, weights)


def turned_body(parts, where_ref, *refs):
    own, outs, rows = refs[:parts], refs[parts:-1], refs[-1]
    chans = own[0].shape[1]
    for j in range(parts):
        shard = lax.rem(where_ref[1] + j, parts)
        rows[pl.ds(pl.multiple_of(shard * chans, chans), chans), :] = own[j][...].T
    pair = where_ref[2] // 2
    for offset, out in enumerate(outs):
        size = out.shape[0]
        out[...] = rows[pl.ds(pl.multiple_of((pair ^ offset) * size, size), size), :]


def turned(where, own, pairs):
    pixels, chans = own[0].shape
    all_chans = len(own) * chans
    whole = pl.BlockSpec(memory_space=pltpu.VMEM)
    return pl.pallas_call(
        functools.partial(turned_body, len(own)),
        out_shape=[jax.ShapeDtypeStruct((all_chans // pairs, pixels), own[0].dtype)] * pairs,
        in_specs=[pl.BlockSpec(memory_space=pltpu.SMEM)] + [whole] * len(own),
        out_specs=[whole] * pairs,
        scratch_shapes=[pltpu.VMEM((all_chans, pixels), own[0].dtype)],
        cost_estimate=pl.CostEstimate(flops=pixels * chans * 64, transcendentals=0, bytes_accessed=4 * pixels * chans),
        name="turned",
    )(where, *own)


def weight_body(blocks, frames, rows, width, clips, scale, where_ref, lens, *refs):
    turned_refs, cots, (out, taps) = refs[:blocks], refs[blocks : 2 * blocks], refs[2 * blocks :]
    chans, pixels = out.shape[1], turned_refs[0].shape[1]
    area = rows * width
    shard = where_ref[2]

    place = lax.broadcasted_iota(jnp.int32, (1, pixels), 1)
    row, col = (place % area) // width, place % width
    masks = {}
    for a in range(SIDE):
        for b in range(SIDE):
            r, c = row + a - 1, col + b - 1
            masks[a, b] = ((r >= 0) & (r < rows) & (c >= 0) & (c < width)).astype(jnp.float32)

    lane = pl.ds(pl.multiple_of((shard % 2) * chans, chans), chans)
    for offset in range(blocks):
        block = shard ^ offset
        value = turned_refs[offset][lane, :].astype(jnp.float32)
        for a in range(SIDE):
            for b in range(SIDE):
                step = (a - 1) * width + b - 1
                copy = value if step == 0 else pltpu.roll(value, (-step) % pixels, 1) * masks[a, b]
                copy = copy.astype(taps.dtype)
                at = (SIDE * a + b) * chans
                for f in range(frames):
                    taps[block * frames + f, at : at + chans] = copy[:, f * area : (f + 1) * area]
    for offset in range(blocks):
        first = (shard ^ offset) * frames

        def lagged(lag, carry, offset=offset, first=first):
            pieces = []
            for f in range(frames):
                frame = first + f
                source = jnp.maximum(frame - lag, first_of(lens, clips, frame))
                pieces.append(taps[source])
            terms = jnp.dot(jnp.concatenate(pieces, axis=1), cots[offset][...], preferred_element_type=jnp.float32)
            at = pl.ds(lag * SIDE * SIDE, SIDE * SIDE)
            terms = terms.reshape(SIDE * SIDE, chans, terms.shape[1])
            if offset == 0:
                out[at] = terms
            elif offset == blocks - 1:
                out[at] = (out[at] + terms) * scale
            else:
                out[at] += terms
            return carry

        lax.fori_loop(0, LAGS, lagged, 0)


def weight_terms(where, lens, turned_blocks, cots, rows, width, scale):
    blocks, pixels = len(cots), cots[0].shape[0]
    chans = turned_blocks[0].shape[0] // 2
    area = rows * width
    frames = pixels // area
    outs = cots[0].shape[1]
    whole = pl.BlockSpec(memory_space=pltpu.VMEM)
    smem = pl.BlockSpec(memory_space=pltpu.SMEM)
    taps = SIDE * SIDE
    return pl.pallas_call(
        functools.partial(weight_body, blocks, frames, rows, width, lens.shape[0], scale),
        out_shape=jax.ShapeDtypeStruct((LAGS * taps, chans, outs), jnp.float32),
        in_specs=[smem, smem] + [whole] * (2 * blocks),
        out_specs=whole,
        scratch_shapes=[pltpu.VMEM((blocks * frames, taps * chans, area), turned_blocks[0].dtype)],
        compiler_params=pltpu.CompilerParams(vmem_limit_bytes=28 << 20),
        cost_estimate=pl.CostEstimate(
            flops=2 * blocks * pixels * LAGS * taps * chans * outs, transcendentals=0, bytes_accessed=8 << 20),
        name="weight_terms",
    )(where, lens, *turned_blocks, *cots)


def extended_2(cells, sides, width):
    for axis, dim in sides:
        count = lax.axis_size(axis)
        ends = count - 1
        head = lax.slice_in_dim(cells, 0, width, axis=dim)
        tail = lax.slice_in_dim(cells, cells.shape[dim] - width, cells.shape[dim], axis=dim)
        cells = jnp.concatenate(
            [
                lax.ppermute(tail, axis, [(i, (i + 1) % count) for i in range(ends)]),
                cells,
                lax.ppermute(head, axis, [((i + 1) % count, i) for i in range(ends)]),
            ],
            axis=dim,
        )
    return cells


def shifted(value, axis, steps):
    count = lax.axis_size(axis)
    leading, last = (max(0, -steps), min(count, count - steps))
    return lax.ppermute(value, axis, [(source, source + steps) for source in range(leading, last)])


def clip_tables(lengths, frame_ids):
    clip_ends = jnp.cumsum(lengths)
    clip_starts = clip_ends - lengths
    clip_ids = jnp.sum((frame_ids[:, None] >= clip_ends[None, :]).astype(jnp.int32), axis=1)
    clip_first = jnp.max(
        jnp.where(clip_starts[None, :] <= frame_ids[:, None], clip_starts[None, :], 0), axis=1
    )
    opening = jnp.any(clip_starts[None, :] == frame_ids[:, None], axis=1)
    return (clip_ids, clip_first, opening)


def input_terms(grad_frames, weights, row_count, col_count):
    frame_total = grad_frames.shape[0]
    local_chans = grad_frames.shape[3]
    all_chans = weights.shape[1]
    pieces = []
    for lag_step in range(3):
        back_stack = jnp.stack(
            [
                grad_frames[
                    :,
                    2 - row_step : 2 - row_step + row_count,
                    2 - col_step : 2 - col_step + col_count,
                    :,
                ]
                for row_step in range(3)
                for col_step in range(3)
            ],
            axis=3,
        ).reshape(frame_total * row_count * col_count, 9 * local_chans)
        back_kernel = jnp.transpose(weights[9 * lag_step : 9 * lag_step + 9], (0, 2, 1)).reshape(
            9 * local_chans, all_chans
        )
        pieces.append(
            jnp.dot(back_stack, back_kernel, preferred_element_type=jnp.float32).reshape(
                frame_total, row_count, col_count, all_chans
            )
        )
    return pieces


def lag_mix(lagged, clip_ids, opening, frame_count):
    here_ids = clip_ids[:frame_count]
    start_flag = opening[:frame_count].astype(jnp.float32)
    act_grad = jnp.zeros((frame_count,) + lagged[0].shape[1:], jnp.float32)
    for lag_step in range(3):
        same_clip = (clip_ids[lag_step : lag_step + frame_count] == here_ids).astype(jnp.float32)
        act_grad = (
            act_grad
            + same_clip[:, None, None, None] * lagged[lag_step][lag_step : lag_step + frame_count]
        )
        for inner_step in range(lag_step):
            near_clip = (clip_ids[inner_step : inner_step + frame_count] == here_ids).astype(
                jnp.float32
            ) * start_flag
            act_grad = (
                act_grad
                + near_clip[:, None, None, None]
                * lagged[lag_step][inner_step : inner_step + frame_count]
            )
    return act_grad


def split_rows(video, channel_gain, weights, lengths, cotangent):
    frame_count, row_count, col_count, local_chans = video.shape
    all_chans = weights.shape[1]
    pixel_count = frame_count * row_count * col_count
    total_pixels = pixel_count * lax.axis_size("tm") * lax.axis_size("rows")
    frame_base = lax.axis_index("tm") * frame_count
    frame_ids = frame_base + jnp.arange(frame_count + 2, dtype=jnp.int32)
    clip_ids, clip_first, opening = clip_tables(lengths, frame_ids)
    own_frames = frame_ids[:frame_count]
    scaled = video.astype(jnp.float32) * channel_gain
    activated = jax.nn.silu(scaled).astype(jnp.bfloat16)
    paired = extended_2(jnp.stack([activated, cotangent]), (("rows", 2),), 1)
    paired = jnp.pad(paired, ((0, 0), (0, 0), (0, 0), (1, 1), (0, 0)))
    act_pad = paired[0]
    grad_pad = paired[1]
    prior_rows = shifted(act_pad, "tm", 1)
    extended = jnp.concatenate([prior_rows, act_pad], axis=0)
    gathered = lax.all_gather(extended, "chan", axis=3, tiled=True)
    flat_grad = cotangent.reshape(pixel_count, local_chans)
    output_sum = jnp.zeros((pixel_count, local_chans), jnp.float32)
    weight_terms = []
    for lag_step in range(3):
        distance = jnp.minimum(lag_step, own_frames - clip_first[:frame_count])[:, None, None, None]
        chosen = jnp.where(
            distance == 0,
            gathered[2 : frame_count + 2],
            jnp.where(distance == 1, gathered[1 : frame_count + 1], gathered[0:frame_count]),
        )
        tap_stack = jnp.stack(
            [
                chosen[:, row_step : row_step + row_count, col_step : col_step + col_count, :]
                for row_step in range(3)
                for col_step in range(3)
            ],
            axis=3,
        ).reshape(pixel_count, 9 * all_chans)
        kernel = weights[9 * lag_step : 9 * lag_step + 9].reshape(9 * all_chans, local_chans)
        output_sum = output_sum + jnp.dot(tap_stack, kernel, preferred_element_type=jnp.float32)
        weight_terms.append(
            lax.dot_general(
                tap_stack, flat_grad, (((0,), (0,)), ((), ())), preferred_element_type=jnp.float32
            ).reshape(9, all_chans, local_chans)
        )
    output = (
        video.astype(jnp.float32)
        + output_sum.reshape(frame_count, row_count, col_count, local_chans)
    ).astype(jnp.bfloat16)
    own_terms = lax.psum_scatter(
        jnp.stack(input_terms(grad_pad, weights, row_count, col_count)),
        "chan",
        scatter_dimension=4,
        tiled=True,
    )
    arriving = shifted(
        jnp.concatenate([own_terms[1, 0:1], own_terms[2, 0:2]], axis=0).astype(jnp.bfloat16),
        "tm",
        -1,
    ).astype(jnp.float32)
    lagged = [
        own_terms[0],
        jnp.concatenate([own_terms[1], arriving[0:1]], axis=0),
        jnp.concatenate([own_terms[2], arriving[1:3]], axis=0),
    ]
    act_grad = lag_mix(lagged, clip_ids, opening, frame_count)
    sigmoid_value = jax.nn.sigmoid(scaled)
    slope_factor = sigmoid_value * (1.0 + scaled * (1.0 - sigmoid_value))
    input_grad = (cotangent.astype(jnp.float32) + act_grad * slope_factor * channel_gain).astype(
        jnp.bfloat16
    )
    weight_sum = jnp.concatenate(weight_terms, axis=0)
    summed = lax.psum_scatter(weight_sum, ("tm", "rows"), scatter_dimension=1, tiled=True)
    weight_grad = summed * (1.0 / math.sqrt(total_pixels))
    return (output, input_grad, weight_grad)


def along(value, axis, steps):
    count = lax.axis_size(axis)
    first, last = max(0, -steps), min(count, count - steps)
    return lax.ppermute(value, axis, [(source, source + steps) for source in range(first, last)])


def across(value, axis, offset):
    return lax.ppermute(value, axis, [(i, i ^ offset) for i in range(lax.axis_size(axis))])


def ahead(value, axis, steps):
    count = lax.axis_size(axis)
    return lax.ppermute(value, axis, [((i + steps) % count, i) for i in range(count)])


def gathered_blocks(own, axis):
    blocks = {0: own}
    bit = lax.axis_size(axis) // 2
    while bit:
        for offset in list(blocks):
            blocks[offset ^ bit] = across(blocks[offset], axis, bit)
        bit //= 2
    return [blocks[offset] for offset in range(len(blocks))]


def whole_rows(video, channel_gain, weights, lengths, cotangent):
    frames, rows, width, chans = video.shape
    all_chans = weights.shape[1]
    parts, shards = all_chans // chans, lax.axis_size("tm")
    pixels = frames * rows * width
    weights = pltpu.with_memory_space_constraint(weights, pltpu.HBM)
    shard, chan = lax.axis_index("tm"), lax.axis_index("chan")
    where = jnp.stack([shard * frames, chan, shard]).astype(jnp.int32)
    scaled = video.astype(jnp.float32) * channel_gain
    activated = silu(video.reshape(pixels, chans), channel_gain).reshape(video.shape)
    own = [activated] + [ahead(activated, "chan", j) for j in range(1, parts)]
    before = along(activated, "tm", 1)
    past = [before] + [ahead(before, "chan", j) for j in range(1, parts)]
    later = along(cotangent, "tm", -1)
    cots = gathered_blocks(cotangent.reshape(pixels, chans), "tm")
    mine, *others = backward(where, lengths, cotangent, later, weights)
    act_grad = mine
    for j in range(1, parts):
        act_grad = act_grad + ahead(others[j - 1], "chan", parts - j).astype(jnp.float32)
    sent = turned(where, [x.reshape(pixels, chans) for x in own], shards // 2)
    blocks = []
    for offset in range(shards // 2):
        block = across(sent[offset], "tm", 2 * offset) if offset else sent[0]
        blocks += [block, across(block, "tm", 1)]
    output = forward(where, lengths, video, own, past, weights)
    sigmoid_value = jax.nn.sigmoid(scaled)
    slope_factor = sigmoid_value * (1.0 + scaled * (1.0 - sigmoid_value))
    input_grad = (cotangent.astype(jnp.float32) + act_grad * slope_factor * channel_gain).astype(jnp.bfloat16)
    scale = 1.0 / math.sqrt(pixels * shards)
    weight_grad = weight_terms(where, lengths, blocks, cots, rows, width, scale)
    return (output, input_grad, weight_grad)


def solution(mesh):
    in_specs = (
        P(("groups", "tm"), "rows", None, "chan"),
        P("chan"),
        P(None, None, "chan"),
        P("groups"),
        P(("groups", "tm"), "rows", None, "chan"),
    )
    out_specs = (
        P(("groups", "tm"), "rows", None, "chan"),
        P(("groups", "tm"), "rows", None, "chan"),
        P("groups", ("tm", "rows"), "chan"),
    )
    body = whole_rows if mesh.shape["rows"] == 1 else split_rows
    return jax.shard_map(body, mesh=mesh, in_specs=in_specs, out_specs=out_specs, check_vma=False)
```

```python
import functools, math
import jax, jax.numpy as jnp
from jax import lax
from jax.experimental import pallas as pl
from jax.experimental.pallas import tpu as pltpu
from jax.sharding import PartitionSpec as P


LAGS = 3
SIDE = 3
PLACES = 3


def first_of(lens, count, frame):
    start, first = jnp.int32(0), jnp.int32(0)
    for i in range(count):
        first = jnp.where(start <= frame, start, first)
        start = start + lens[i]
    return first


def opens(lens, count, frame):
    start, hit = jnp.int32(0), jnp.int32(0)
    for i in range(count):
        hit = jnp.where(start == frame, 1, hit)
        start = start + lens[i]
    return hit


def joined(lens, count, frame, later):
    end, cut = jnp.int32(0), jnp.int32(0)
    for i in range(count):
        end = end + lens[i]
        cut = jnp.where((frame < end) & (end <= later), 1, cut)
    return 1 - cut


def moved(value, steps, width):
    rows = value.shape[0]
    col = lax.broadcasted_iota(jnp.int32, value.shape, 0) % width
    if steps == 1:
        return jnp.where(col == width - 1, 0.0, pltpu.roll(value, rows - 1, 0))
    return jnp.where(col == 0, 0.0, pltpu.roll(value, 1, 0))


def silu_body(video, gain, out):
    scaled = video[...].astype(jnp.float32) * gain[...]
    out[...] = (scaled / (1.0 + jnp.exp(-scaled))).astype(out.dtype)


def silu(video, gain):
    whole = pl.BlockSpec(memory_space=pltpu.VMEM)
    return pl.pallas_call(
        silu_body,
        out_shape=jax.ShapeDtypeStruct(video.shape, video.dtype),
        in_specs=[whole, whole],
        out_specs=whole,
        compiler_params=pltpu.CompilerParams(vmem_limit_bytes=4 << 20),
        cost_estimate=pl.CostEstimate(flops=8 * video.size, transcendentals=video.size, bytes_accessed=4 * video.size),
        name="silu",
    )(video, gain.reshape(1, -1))


def fetch(weights, held, sems):
    for row_step in range(SIDE):
        for lag in range(LAGS):
            for b in range(SIDE):
                tap = SIDE * (SIDE * lag + row_step) + b
                pltpu.make_async_copy(weights.at[tap], held.at[tap], sems.at[tap]).start()


def arrived(weights, held, sems, row_step):
    for lag in range(LAGS):
        for b in range(SIDE):
            tap = SIDE * (SIDE * lag + row_step) + b
            pltpu.make_async_copy(weights.at[tap], held.at[tap], sems.at[tap]).wait()


def forward_body(parts, clips, where_ref, video, *refs):
    own, past = refs[:parts], refs[parts : 2 * parts]
    weights, out, padded, acc, held, sems = refs[2 * parts :]
    frames, rows, width, chans = video.shape
    base, chan = where_ref[0], where_ref[1]
    lens = [where_ref[PLACES + i] for i in range(clips)]
    fetch(weights, held, sems)
    edge = jnp.zeros((2 * frames, 1, width, chans), padded.dtype)
    for j in range(parts):
        shard = lax.rem(chan + j, parts)
        padded[shard, :, 0:1] = edge
        padded[shard, :, rows + 1 : rows + 2] = edge
        padded[shard, 0:frames, 1 : rows + 1] = past[j][...]
        padded[shard, frames : 2 * frames, 1 : rows + 1] = own[j][...]
    acc[...] = jnp.zeros_like(acc)

    def step(row_step, carry):
        arrived(weights, held, sems, row_step)
        taps = []
        for f in range(frames):
            frame = base + f
            pieces = []
            for lag in range(LAGS):
                source = jnp.maximum(frame - lag, first_of(lens, clips, frame)) - base + frames
                for j in range(parts):
                    pieces.append(padded[j, source, pl.ds(row_step, rows)].reshape(rows * width, chans))
            taps.append(jnp.concatenate(pieces, axis=1))
        taps = jnp.concatenate(taps, axis=0)
        for b in range(SIDE):
            kernel = jnp.concatenate([held[SIDE * (SIDE * lag + row_step) + b] for lag in range(LAGS)], axis=0)
            acc[b] += jnp.dot(taps, kernel, preferred_element_type=jnp.float32)
        return carry

    lax.fori_loop(0, SIDE, step, 0)
    total = acc[1] + moved(acc[0], -1, width) + moved(acc[2], 1, width)
    out[...] = (video[...].astype(jnp.float32) + total.reshape(video.shape)).astype(out.dtype)


def forward(where, video, own, past, weights):
    frames, rows, width, chans = video.shape
    parts, pixels = len(own), frames * rows * width
    whole = pl.BlockSpec(memory_space=pltpu.VMEM)
    smem = pl.BlockSpec(memory_space=pltpu.SMEM)
    return pl.pallas_call(
        functools.partial(forward_body, parts, where.shape[0] - PLACES),
        out_shape=jax.ShapeDtypeStruct(video.shape, video.dtype),
        in_specs=[smem, whole] + [whole] * (2 * parts) + [pl.BlockSpec(memory_space=pltpu.HBM)],
        out_specs=whole,
        scratch_shapes=[
            pltpu.VMEM((parts, 2 * frames, rows + 2, width, chans), video.dtype),
            pltpu.VMEM((SIDE, pixels, weights.shape[2]), jnp.float32),
            pltpu.VMEM(weights.shape, weights.dtype),
            pltpu.SemaphoreType.DMA((weights.shape[0],)),
        ],
        compiler_params=pltpu.CompilerParams(vmem_limit_bytes=20 << 20),
        cost_estimate=pl.CostEstimate(
            flops=2 * pixels * weights.size, transcendentals=0, bytes_accessed=2 * weights.size),
        name="forward",
    )(where, video, *own, *past, weights)


def backward_body(parts, clips, where_ref, own, later, weights, mine, *refs):
    others, (mixed, acc, held, sems) = refs[: parts - 1], refs[parts - 1 :]
    frames, rows, width, chans = own.shape
    pixels = frames * rows * width
    base, chan = where_ref[0], where_ref[1]
    lens = [where_ref[PLACES + i] for i in range(clips)]
    fetch(weights, held, sems)
    mixed[:, :, 0:1] = jnp.zeros((LAGS, frames, 1, width, chans), mixed.dtype)
    mixed[:, :, rows + 1 : rows + 2] = jnp.zeros((LAGS, frames, 1, width, chans), mixed.dtype)
    take = lambda f: (own[f] if f < frames else later[f - frames]).astype(jnp.float32)
    for f in range(frames):
        frame = base + f
        start = opens(lens, clips, frame).astype(jnp.float32)
        next_one = joined(lens, clips, frame, frame + 1).astype(jnp.float32)
        next_two = joined(lens, clips, frame, frame + 2).astype(jnp.float32)
        mixed[0, f, 1 : rows + 1] = own[f]
        mixed[1, f, 1 : rows + 1] = (next_one * take(f + 1) + start * take(f)).astype(mixed.dtype)
        mixed[2, f, 1 : rows + 1] = (
            next_two * take(f + 2) + start * (take(f) + next_one * take(f + 1))
        ).astype(mixed.dtype)
    acc[...] = jnp.zeros_like(acc)

    def step(row_step, carry):
        arrived(weights, held, sems, row_step)
        taps = [mixed[lag, :, pl.ds(2 - row_step, rows)].reshape(pixels, chans) for lag in range(LAGS)]
        taps = jnp.concatenate(taps, axis=1)
        for b in range(SIDE):
            kernel = jnp.concatenate([held[SIDE * (SIDE * lag + row_step) + b] for lag in range(LAGS)], axis=1)
            acc[b] += lax.dot_general(taps, kernel, (((1,), (1,)), ((), ())), preferred_element_type=jnp.float32)
        return carry

    lax.fori_loop(0, SIDE, step, 0)
    for j in range(parts):
        at = pl.ds(pl.multiple_of(lax.rem(chan + j, parts) * chans, chans), chans)
        total = acc[1, :, at] + moved(acc[0, :, at], 1, width) + moved(acc[2, :, at], -1, width)
        if j == 0:
            mine[...] = total.reshape(mine.shape)
        else:
            others[j - 1][...] = total.reshape(mine.shape).astype(others[j - 1].dtype)


def backward(where, own, later, weights):
    frames, rows, width, chans = own.shape
    parts, pixels = weights.shape[1] // chans, frames * rows * width
    whole = pl.BlockSpec(memory_space=pltpu.VMEM)
    smem = pl.BlockSpec(memory_space=pltpu.SMEM)
    return pl.pallas_call(
        functools.partial(backward_body, parts, where.shape[0] - PLACES),
        out_shape=[jax.ShapeDtypeStruct(own.shape, jnp.float32)]
        + [jax.ShapeDtypeStruct(own.shape, own.dtype)] * (parts - 1),
        in_specs=[smem, whole, whole, pl.BlockSpec(memory_space=pltpu.HBM)],
        out_specs=[whole] * parts,
        scratch_shapes=[
            pltpu.VMEM((LAGS, frames, rows + 2, width, chans), own.dtype),
            pltpu.VMEM((SIDE, pixels, parts * chans), jnp.float32),
            pltpu.VMEM(weights.shape, weights.dtype),
            pltpu.SemaphoreType.DMA((weights.shape[0],)),
        ],
        compiler_params=pltpu.CompilerParams(vmem_limit_bytes=20 << 20),
        cost_estimate=pl.CostEstimate(
            flops=2 * pixels * weights.size, transcendentals=0, bytes_accessed=2 * weights.size),
        name="backward",
    )(where, own, later, weights)


def turned_body(parts, where_ref, *refs):
    own, outs, rows = refs[:parts], refs[parts:-1], refs[-1]
    chans = own[0].shape[1]
    for j in range(parts):
        shard = lax.rem(where_ref[1] + j, parts)
        rows[pl.ds(pl.multiple_of(shard * chans, chans), chans), :] = own[j][...].T
    pair = where_ref[2] // 2
    for offset, out in enumerate(outs):
        size = out.shape[0]
        out[...] = rows[pl.ds(pl.multiple_of((pair ^ offset) * size, size), size), :]


def turned(where, own, pairs):
    pixels, chans = own[0].shape
    all_chans = len(own) * chans
    whole = pl.BlockSpec(memory_space=pltpu.VMEM)
    return pl.pallas_call(
        functools.partial(turned_body, len(own)),
        out_shape=[jax.ShapeDtypeStruct((all_chans // pairs, pixels), own[0].dtype)] * pairs,
        in_specs=[pl.BlockSpec(memory_space=pltpu.SMEM)] + [whole] * len(own),
        out_specs=[whole] * pairs,
        scratch_shapes=[pltpu.VMEM((all_chans, pixels), own[0].dtype)],
        compiler_params=pltpu.CompilerParams(vmem_limit_bytes=4 << 20),
        cost_estimate=pl.CostEstimate(flops=pixels * chans * 64, transcendentals=0, bytes_accessed=4 * pixels * chans),
        name="turned",
    )(where, *own)


def weight_body(blocks, group, rows, width, clips, scale, where_ref, *refs):
    turned_refs, cots, (out, taps) = refs[:blocks], refs[blocks : 2 * blocks], refs[2 * blocks :]
    pixels = turned_refs[0].shape[1]
    area, chans, outs = rows * width, out.shape[3], out.shape[4]
    frames = pixels // area
    shard = where_ref[2]
    lens = [where_ref[PLACES + i] for i in range(clips)]
    col = lax.broadcasted_iota(jnp.int32, (1, pixels), 1) % width
    left, right = (col > 0).astype(jnp.float32), (col < width - 1).astype(jnp.float32)

    lane = pl.ds(pl.multiple_of((shard % 2) * chans, chans), chans)
    for offset in range(blocks):
        block = shard ^ offset
        value = turned_refs[offset][lane, :].astype(jnp.float32)
        copies = (pltpu.roll(value, 1, 1) * left, value, pltpu.roll(value, pixels - 1, 1) * right)
        for b, copy in enumerate(copies):
            copy = copy.astype(taps.dtype)
            for f in range(frames):
                taps[block * frames + f, b * chans : (b + 1) * chans] = copy[:, f * area : (f + 1) * area]
    edge = jnp.zeros((width, outs), cots[0].dtype)
    for start in range(0, blocks, group):
        offsets = range(start, start + group)
        pieces = []
        for offset in offsets:
            for f in range(frames):
                frame = (shard ^ offset) * frames + f
                first = first_of(lens, clips, frame)
                sources = [jnp.maximum(frame - lag, first) for lag in range(LAGS)]
                pieces.append(jnp.concatenate([taps[source] for source in sources], axis=0))
        pieces = jnp.concatenate(pieces, axis=1)
        for row_step in range(SIDE):
            values = []
            for offset in offsets:
                for f in range(frames):
                    top, end = f * area, (f + 1) * area
                    if row_step == 0:
                        values += [cots[offset][top + width : end], edge]
                    elif row_step == 1:
                        values += [cots[offset][top:end]]
                    else:
                        values += [edge, cots[offset][top : end - width]]
            terms = jnp.dot(pieces, jnp.concatenate(values, axis=0), preferred_element_type=jnp.float32)
            terms = terms.reshape(LAGS, SIDE, chans, outs)
            if start:
                terms = terms + out[:, row_step]
            out[:, row_step] = terms * scale if start + group == blocks else terms


def weight_terms(where, turned_blocks, cots, rows, width, scale, group=2):
    blocks, pixels = len(cots), cots[0].shape[0]
    chans = turned_blocks[0].shape[0] // 2
    outs = cots[0].shape[1]
    whole = pl.BlockSpec(memory_space=pltpu.VMEM)
    smem = pl.BlockSpec(memory_space=pltpu.SMEM)
    taps = LAGS * SIDE * SIDE
    frames = pixels // (rows * width)
    result = pl.pallas_call(
        functools.partial(weight_body, blocks, group, rows, width, where.shape[0] - PLACES, scale),
        out_shape=jax.ShapeDtypeStruct((LAGS, SIDE, SIDE, chans, outs), jnp.float32),
        in_specs=[smem] + [whole] * (2 * blocks),
        out_specs=whole,
        scratch_shapes=[pltpu.VMEM((blocks * frames, SIDE * chans, rows * width), turned_blocks[0].dtype)],
        compiler_params=pltpu.CompilerParams(vmem_limit_bytes=8 << 20),
        cost_estimate=pl.CostEstimate(
            flops=2 * blocks * pixels * taps * chans * outs, transcendentals=0, bytes_accessed=8 << 20),
        name="weight_terms",
    )(where, *turned_blocks, *cots)
    return result.reshape(taps, chans, outs)


def extended_2(cells, sides, width):
    for axis, dim in sides:
        count = lax.axis_size(axis)
        ends = count - 1
        head = lax.slice_in_dim(cells, 0, width, axis=dim)
        tail = lax.slice_in_dim(cells, cells.shape[dim] - width, cells.shape[dim], axis=dim)
        cells = jnp.concatenate(
            [
                lax.ppermute(tail, axis, [(i, (i + 1) % count) for i in range(ends)]),
                cells,
                lax.ppermute(head, axis, [((i + 1) % count, i) for i in range(ends)]),
            ],
            axis=dim,
        )
    return cells


def shifted(value, axis, steps):
    count = lax.axis_size(axis)
    leading, last = (max(0, -steps), min(count, count - steps))
    return lax.ppermute(value, axis, [(source, source + steps) for source in range(leading, last)])


def clip_tables(lengths, frame_ids):
    clip_ends = jnp.cumsum(lengths)
    clip_starts = clip_ends - lengths
    clip_ids = jnp.sum((frame_ids[:, None] >= clip_ends[None, :]).astype(jnp.int32), axis=1)
    clip_first = jnp.max(
        jnp.where(clip_starts[None, :] <= frame_ids[:, None], clip_starts[None, :], 0), axis=1
    )
    opening = jnp.any(clip_starts[None, :] == frame_ids[:, None], axis=1)
    return (clip_ids, clip_first, opening)


def input_terms(grad_frames, weights, row_count, col_count):
    frame_total = grad_frames.shape[0]
    local_chans = grad_frames.shape[3]
    all_chans = weights.shape[1]
    pieces = []
    for lag_step in range(3):
        back_stack = jnp.stack(
            [
                grad_frames[
                    :,
                    2 - row_step : 2 - row_step + row_count,
                    2 - col_step : 2 - col_step + col_count,
                    :,
                ]
                for row_step in range(3)
                for col_step in range(3)
            ],
            axis=3,
        ).reshape(frame_total * row_count * col_count, 9 * local_chans)
        back_kernel = jnp.transpose(weights[9 * lag_step : 9 * lag_step + 9], (0, 2, 1)).reshape(
            9 * local_chans, all_chans
        )
        pieces.append(
            jnp.dot(back_stack, back_kernel, preferred_element_type=jnp.float32).reshape(
                frame_total, row_count, col_count, all_chans
            )
        )
    return pieces


def lag_mix(lagged, clip_ids, opening, frame_count):
    here_ids = clip_ids[:frame_count]
    start_flag = opening[:frame_count].astype(jnp.float32)
    act_grad = jnp.zeros((frame_count,) + lagged[0].shape[1:], jnp.float32)
    for lag_step in range(3):
        same_clip = (clip_ids[lag_step : lag_step + frame_count] == here_ids).astype(jnp.float32)
        act_grad = (
            act_grad
            + same_clip[:, None, None, None] * lagged[lag_step][lag_step : lag_step + frame_count]
        )
        for inner_step in range(lag_step):
            near_clip = (clip_ids[inner_step : inner_step + frame_count] == here_ids).astype(
                jnp.float32
            ) * start_flag
            act_grad = (
                act_grad
                + near_clip[:, None, None, None]
                * lagged[lag_step][inner_step : inner_step + frame_count]
            )
    return act_grad


def split_rows(video, channel_gain, weights, lengths, cotangent):
    frame_count, row_count, col_count, local_chans = video.shape
    all_chans = weights.shape[1]
    pixel_count = frame_count * row_count * col_count
    total_pixels = pixel_count * lax.axis_size("tm") * lax.axis_size("rows")
    frame_base = lax.axis_index("tm") * frame_count
    frame_ids = frame_base + jnp.arange(frame_count + 2, dtype=jnp.int32)
    clip_ids, clip_first, opening = clip_tables(lengths, frame_ids)
    own_frames = frame_ids[:frame_count]
    scaled = video.astype(jnp.float32) * channel_gain
    activated = jax.nn.silu(scaled).astype(jnp.bfloat16)
    paired = extended_2(jnp.stack([activated, cotangent]), (("rows", 2),), 1)
    paired = jnp.pad(paired, ((0, 0), (0, 0), (0, 0), (1, 1), (0, 0)))
    act_pad = paired[0]
    grad_pad = paired[1]
    prior_rows = shifted(act_pad, "tm", 1)
    extended = jnp.concatenate([prior_rows, act_pad], axis=0)
    gathered = lax.all_gather(extended, "chan", axis=3, tiled=True)
    flat_grad = cotangent.reshape(pixel_count, local_chans)
    output_sum = jnp.zeros((pixel_count, local_chans), jnp.float32)
    weight_terms = []
    for lag_step in range(3):
        distance = jnp.minimum(lag_step, own_frames - clip_first[:frame_count])[:, None, None, None]
        chosen = jnp.where(
            distance == 0,
            gathered[2 : frame_count + 2],
            jnp.where(distance == 1, gathered[1 : frame_count + 1], gathered[0:frame_count]),
        )
        tap_stack = jnp.stack(
            [
                chosen[:, row_step : row_step + row_count, col_step : col_step + col_count, :]
                for row_step in range(3)
                for col_step in range(3)
            ],
            axis=3,
        ).reshape(pixel_count, 9 * all_chans)
        kernel = weights[9 * lag_step : 9 * lag_step + 9].reshape(9 * all_chans, local_chans)
        output_sum = output_sum + jnp.dot(tap_stack, kernel, preferred_element_type=jnp.float32)
        weight_terms.append(
            lax.dot_general(
                tap_stack, flat_grad, (((0,), (0,)), ((), ())), preferred_element_type=jnp.float32
            ).reshape(9, all_chans, local_chans)
        )
    output = (
        video.astype(jnp.float32)
        + output_sum.reshape(frame_count, row_count, col_count, local_chans)
    ).astype(jnp.bfloat16)
    own_terms = lax.psum_scatter(
        jnp.stack(input_terms(grad_pad, weights, row_count, col_count)),
        "chan",
        scatter_dimension=4,
        tiled=True,
    )
    arriving = shifted(
        jnp.concatenate([own_terms[1, 0:1], own_terms[2, 0:2]], axis=0).astype(jnp.bfloat16),
        "tm",
        -1,
    ).astype(jnp.float32)
    lagged = [
        own_terms[0],
        jnp.concatenate([own_terms[1], arriving[0:1]], axis=0),
        jnp.concatenate([own_terms[2], arriving[1:3]], axis=0),
    ]
    act_grad = lag_mix(lagged, clip_ids, opening, frame_count)
    sigmoid_value = jax.nn.sigmoid(scaled)
    slope_factor = sigmoid_value * (1.0 + scaled * (1.0 - sigmoid_value))
    input_grad = (cotangent.astype(jnp.float32) + act_grad * slope_factor * channel_gain).astype(
        jnp.bfloat16
    )
    weight_sum = jnp.concatenate(weight_terms, axis=0)
    summed = lax.psum_scatter(weight_sum, ("tm", "rows"), scatter_dimension=1, tiled=True)
    weight_grad = summed * (1.0 / math.sqrt(total_pixels))
    return (output, input_grad, weight_grad)


def along(value, axis, steps):
    count = lax.axis_size(axis)
    first, last = max(0, -steps), min(count, count - steps)
    return lax.ppermute(value, axis, [(source, source + steps) for source in range(first, last)])


def across(value, axis, offset):
    return lax.ppermute(value, axis, [(i, i ^ offset) for i in range(lax.axis_size(axis))])


def ahead(value, axis, steps):
    count = lax.axis_size(axis)
    return lax.ppermute(value, axis, [((i + steps) % count, i) for i in range(count)])


def gathered_blocks(own, axis):
    blocks = {0: own}
    bit = lax.axis_size(axis) // 2
    while bit:
        for offset in list(blocks):
            blocks[offset ^ bit] = across(blocks[offset], axis, bit)
        bit //= 2
    return [blocks[offset] for offset in range(len(blocks))]


def whole_rows(video, channel_gain, weights, lengths, cotangent):
    frames, rows, width, chans = video.shape
    all_chans = weights.shape[1]
    parts, shards = all_chans // chans, lax.axis_size("tm")
    pixels = frames * rows * width
    weights = pltpu.with_memory_space_constraint(weights, pltpu.HBM)
    shard, chan = lax.axis_index("tm"), lax.axis_index("chan")
    where = jnp.concatenate([jnp.stack([shard * frames, chan, shard]), lengths]).astype(jnp.int32)
    scaled = video.astype(jnp.float32) * channel_gain
    activated = silu(video.reshape(pixels, chans), channel_gain).reshape(video.shape)
    own = [activated] + [ahead(activated, "chan", j) for j in range(1, parts)]
    before = along(activated, "tm", 1)
    past = [before] + [ahead(before, "chan", j) for j in range(1, parts)]
    later = along(cotangent, "tm", -1)
    cots = gathered_blocks(cotangent.reshape(pixels, chans), "tm")
    mine, *others = backward(where, cotangent, later, weights)
    act_grad = mine
    for j in range(1, parts):
        act_grad = act_grad + ahead(others[j - 1], "chan", parts - j).astype(jnp.float32)
    sent = turned(where, [x.reshape(pixels, chans) for x in own], shards // 2)
    blocks = []
    for offset in range(shards // 2):
        block = across(sent[offset], "tm", 2 * offset) if offset else sent[0]
        blocks += [block, across(block, "tm", 1)]
    output = forward(where, video, own, past, weights)
    sigmoid_value = jax.nn.sigmoid(scaled)
    slope_factor = sigmoid_value * (1.0 + scaled * (1.0 - sigmoid_value))
    input_grad = (cotangent.astype(jnp.float32) + act_grad * slope_factor * channel_gain).astype(jnp.bfloat16)
    scale = 1.0 / math.sqrt(pixels * shards)
    weight_grad = weight_terms(where, blocks, cots, rows, width, scale)
    return (output, input_grad, weight_grad)


def solution(mesh):
    in_specs = (
        P(("groups", "tm"), "rows", None, "chan"),
        P("chan"),
        P(None, None, "chan"),
        P("groups"),
        P(("groups", "tm"), "rows", None, "chan"),
    )
    out_specs = (
        P(("groups", "tm"), "rows", None, "chan"),
        P(("groups", "tm"), "rows", None, "chan"),
        P("groups", ("tm", "rows"), "chan"),
    )
    body = whole_rows if mesh.shape["rows"] == 1 else split_rows
    return jax.shard_map(body, mesh=mesh, in_specs=in_specs, out_specs=out_specs, check_vma=False)
```

```python
import functools, math
import jax, jax.numpy as jnp
from jax import lax
from jax.experimental import pallas as pl
from jax.experimental.pallas import tpu as pltpu
from jax.sharding import PartitionSpec as P


LAGS = 3
SIDE = 3
PLACES = 3


def first_of(lens, count, frame):
    start, first = jnp.int32(0), jnp.int32(0)
    for i in range(count):
        first = jnp.where(start <= frame, start, first)
        start = start + lens[i]
    return first


def opens(lens, count, frame):
    start, hit = jnp.int32(0), jnp.int32(0)
    for i in range(count):
        hit = jnp.where(start == frame, 1, hit)
        start = start + lens[i]
    return hit


def joined(lens, count, frame, later):
    end, cut = jnp.int32(0), jnp.int32(0)
    for i in range(count):
        end = end + lens[i]
        cut = jnp.where((frame < end) & (end <= later), 1, cut)
    return 1 - cut


def moved(value, steps, width):
    rows = value.shape[0]
    col = lax.broadcasted_iota(jnp.int32, value.shape, 0) % width
    if steps == 1:
        return jnp.where(col == width - 1, 0.0, pltpu.roll(value, rows - 1, 0))
    return jnp.where(col == 0, 0.0, pltpu.roll(value, 1, 0))


def silu_body(video, gain, out):
    scaled = video[...].astype(jnp.float32) * gain[...]
    out[...] = (scaled / (1.0 + jnp.exp(-scaled))).astype(out.dtype)


def silu(video, gain):
    whole = pl.BlockSpec(memory_space=pltpu.VMEM)
    return pl.pallas_call(
        silu_body,
        out_shape=jax.ShapeDtypeStruct(video.shape, video.dtype),
        in_specs=[whole, whole],
        out_specs=whole,
        compiler_params=pltpu.CompilerParams(vmem_limit_bytes=4 << 20),
        cost_estimate=pl.CostEstimate(flops=8 * video.size, transcendentals=video.size, bytes_accessed=4 * video.size),
        name="silu",
    )(video, gain.reshape(1, -1))


def forward_body(parts, clips, where_ref, video, *refs):
    own, past = refs[:parts], refs[parts : 2 * parts]
    weights, out, padded, acc = refs[2 * parts :]
    frames, rows, width, chans = video.shape
    base, chan = where_ref[0], where_ref[1]
    lens = [where_ref[PLACES + i] for i in range(clips)]
    edge = jnp.zeros((2 * frames, 1, width, chans), padded.dtype)
    for j in range(parts):
        shard = lax.rem(chan + j, parts)
        padded[shard, :, 0:1] = edge
        padded[shard, :, rows + 1 : rows + 2] = edge
        padded[shard, 0:frames, 1 : rows + 1] = past[j][...]
        padded[shard, frames : 2 * frames, 1 : rows + 1] = own[j][...]

    def step(row_step, carry):
        taps = []
        for f in range(frames):
            frame = base + f
            first = first_of(lens, clips, frame)
            pieces = []
            for lag in range(LAGS):
                source = jnp.maximum(frame - lag, first) - base + frames
                for j in range(parts):
                    pieces.append(padded[j, source, pl.ds(row_step, rows)].reshape(rows * width, chans))
            taps.append(jnp.concatenate(pieces, axis=1))
        taps = jnp.concatenate(taps, axis=0)
        for b in range(SIDE):
            kernel = jnp.concatenate([weights[SIDE * (SIDE * lag + row_step) + b] for lag in range(LAGS)], axis=0)
            terms = jnp.dot(taps, kernel, preferred_element_type=jnp.float32)
            acc[b] += terms
        return carry

    acc[...] = jnp.zeros_like(acc)
    lax.fori_loop(0, SIDE, step, 0)
    total = acc[1] + moved(acc[0], -1, width) + moved(acc[2], 1, width)
    out[...] = (video[...].astype(jnp.float32) + total.reshape(video.shape)).astype(out.dtype)


def forward(where, video, own, past, weights):
    frames, rows, width, chans = video.shape
    parts, pixels = len(own), frames * rows * width
    whole = pl.BlockSpec(memory_space=pltpu.VMEM)
    smem = pl.BlockSpec(memory_space=pltpu.SMEM)
    return pl.pallas_call(
        functools.partial(forward_body, parts, where.shape[0] - PLACES),
        out_shape=jax.ShapeDtypeStruct(video.shape, video.dtype),
        in_specs=[smem, whole] + [whole] * (2 * parts) + [whole],
        out_specs=whole,
        scratch_shapes=[
            pltpu.VMEM((parts, 2 * frames, rows + 2, width, chans), video.dtype),
            pltpu.VMEM((SIDE, pixels, weights.shape[2]), jnp.float32),
        ],
        compiler_params=pltpu.CompilerParams(vmem_limit_bytes=10 << 20),
        cost_estimate=pl.CostEstimate(
            flops=2 * pixels * weights.size, transcendentals=0, bytes_accessed=2 * weights.size),
        name="forward",
    )(where, video, *own, *past, weights)


def backward_body(parts, clips, where_ref, own, later, weights, mine, *refs):
    others, (mixed, acc) = refs[: parts - 1], refs[parts - 1 :]
    frames, rows, width, chans = own.shape
    pixels = frames * rows * width
    base, chan = where_ref[0], where_ref[1]
    lens = [where_ref[PLACES + i] for i in range(clips)]
    mixed[:, :, 0:1] = jnp.zeros((LAGS, frames, 1, width, chans), mixed.dtype)
    mixed[:, :, rows + 1 : rows + 2] = jnp.zeros((LAGS, frames, 1, width, chans), mixed.dtype)
    take = lambda f: (own[f] if f < frames else later[f - frames]).astype(jnp.float32)
    for f in range(frames):
        frame = base + f
        start = opens(lens, clips, frame).astype(jnp.float32)
        next_one = joined(lens, clips, frame, frame + 1).astype(jnp.float32)
        next_two = joined(lens, clips, frame, frame + 2).astype(jnp.float32)
        mixed[0, f, 1 : rows + 1] = own[f]
        mixed[1, f, 1 : rows + 1] = (next_one * take(f + 1) + start * take(f)).astype(mixed.dtype)
        mixed[2, f, 1 : rows + 1] = (
            next_two * take(f + 2) + start * (take(f) + next_one * take(f + 1))
        ).astype(mixed.dtype)

    def step(row_step, carry):
        taps = [mixed[lag, :, pl.ds(2 - row_step, rows)].reshape(pixels, chans) for lag in range(LAGS)]
        taps = jnp.concatenate(taps, axis=1)
        for b in range(SIDE):
            kernel = jnp.concatenate([weights[SIDE * (SIDE * lag + row_step) + b] for lag in range(LAGS)], axis=1)
            terms = lax.dot_general(taps, kernel, (((1,), (1,)), ((), ())), preferred_element_type=jnp.float32)
            acc[b] += terms
        return carry

    acc[...] = jnp.zeros_like(acc)
    lax.fori_loop(0, SIDE, step, 0)
    for j in range(parts):
        at = pl.ds(pl.multiple_of(lax.rem(chan + j, parts) * chans, chans), chans)
        total = acc[1, :, at] + moved(acc[0, :, at], 1, width) + moved(acc[2, :, at], -1, width)
        if j == 0:
            mine[...] = total.reshape(mine.shape)
        else:
            others[j - 1][...] = total.reshape(mine.shape).astype(others[j - 1].dtype)


def backward(where, own, later, weights):
    frames, rows, width, chans = own.shape
    parts, pixels = weights.shape[1] // chans, frames * rows * width
    whole = pl.BlockSpec(memory_space=pltpu.VMEM)
    smem = pl.BlockSpec(memory_space=pltpu.SMEM)
    return pl.pallas_call(
        functools.partial(backward_body, parts, where.shape[0] - PLACES),
        out_shape=[jax.ShapeDtypeStruct(own.shape, jnp.float32)]
        + [jax.ShapeDtypeStruct(own.shape, own.dtype)] * (parts - 1),
        in_specs=[smem, whole, whole, whole],
        out_specs=[whole] * parts,
        scratch_shapes=[
            pltpu.VMEM((LAGS, frames, rows + 2, width, chans), own.dtype),
            pltpu.VMEM((SIDE, pixels, parts * chans), jnp.float32),
        ],
        compiler_params=pltpu.CompilerParams(vmem_limit_bytes=10 << 20),
        cost_estimate=pl.CostEstimate(
            flops=2 * pixels * weights.size, transcendentals=0, bytes_accessed=2 * weights.size),
        name="backward",
    )(where, own, later, weights)


def turned_body(parts, where_ref, *refs):
    own, (*outs, rows) = refs[:parts], refs[parts:]
    chans = own[0].shape[1]
    for j in range(parts):
        shard = lax.rem(where_ref[1] + j, parts)
        rows[pl.ds(pl.multiple_of(shard * chans, chans), chans), :] = own[j][...].T
    pair = where_ref[2] // 2
    for offset, out in enumerate(outs):
        size = out.shape[0]
        out[...] = rows[pl.ds(pl.multiple_of((pair ^ offset) * size, size), size), :]


def turned(where, own, pairs):
    pixels, chans = own[0].shape
    all_chans = len(own) * chans
    whole = pl.BlockSpec(memory_space=pltpu.VMEM)
    return pl.pallas_call(
        functools.partial(turned_body, len(own)),
        out_shape=[jax.ShapeDtypeStruct((all_chans // pairs, pixels), own[0].dtype)] * pairs,
        in_specs=[pl.BlockSpec(memory_space=pltpu.SMEM)] + [whole] * len(own),
        out_specs=[whole] * pairs,
        scratch_shapes=[pltpu.VMEM((all_chans, pixels), own[0].dtype)],
        compiler_params=pltpu.CompilerParams(vmem_limit_bytes=4 << 20),
        cost_estimate=pl.CostEstimate(flops=4 << 30, transcendentals=0, bytes_accessed=4 * pixels * chans),
        name="turned",
    )(where, *own)


def weight_body(blocks, group, rows, width, clips, scale, where_ref, video, gain, mine, *refs):
    turned_refs, cots = refs[:blocks], refs[blocks : 2 * blocks]
    *others, out, input_grad, taps = refs[2 * blocks :]
    pixels = turned_refs[0].shape[1]
    area, chans, outs = rows * width, out.shape[3], out.shape[4]
    frames = pixels // area
    shard = where_ref[2]
    lens = [where_ref[PLACES + i] for i in range(clips)]
    col = lax.broadcasted_iota(jnp.int32, (1, pixels), 1) % width
    left, right = (col > 0).astype(jnp.float32), (col < width - 1).astype(jnp.float32)

    lane = pl.ds(pl.multiple_of((shard % 2) * chans, chans), chans)
    for offset in range(blocks):
        block = shard ^ offset
        value = turned_refs[offset][lane, :].astype(jnp.float32)
        copies = (pltpu.roll(value, 1, 1) * left, value, pltpu.roll(value, pixels - 1, 1) * right)
        for b, copy in enumerate(copies):
            copy = copy.astype(taps.dtype)
            for f in range(frames):
                taps[block * frames + f, b * chans : (b + 1) * chans] = copy[:, f * area : (f + 1) * area]
    edge = jnp.zeros((width, outs), cots[0].dtype)
    for start in range(0, blocks, group):
        offsets = range(start, start + group)
        pieces = []
        for offset in offsets:
            for f in range(frames):
                frame = (shard ^ offset) * frames + f
                first = first_of(lens, clips, frame)
                sources = [jnp.maximum(frame - lag, first) for lag in range(LAGS)]
                pieces.append(jnp.concatenate([taps[source] for source in sources], axis=0))
        pieces = jnp.concatenate(pieces, axis=1)
        if start + group == blocks:
            act_grad = mine[...]
            for other in others:
                act_grad = act_grad + other[...].astype(jnp.float32)
            scaled = video[...].astype(jnp.float32) * gain[...]
            sigmoid = 1.0 / (1.0 + jnp.exp(-scaled))
            slope = sigmoid * (1.0 + scaled * (1.0 - sigmoid))
            total = cots[0][...].astype(jnp.float32) + act_grad * slope * gain[...]
            input_grad[...] = total.astype(input_grad.dtype)
        for row_step in range(SIDE):
            values = []
            for offset in offsets:
                for f in range(frames):
                    top, end = f * area, (f + 1) * area
                    if row_step == 0:
                        values += [cots[offset][top + width : end], edge]
                    elif row_step == 1:
                        values += [cots[offset][top:end]]
                    else:
                        values += [edge, cots[offset][top : end - width]]
            terms = jnp.dot(pieces, jnp.concatenate(values, axis=0), preferred_element_type=jnp.float32)
            terms = terms.reshape(LAGS, SIDE, chans, outs)
            if start:
                terms = terms + out[:, row_step]
            out[:, row_step] = terms * scale if start + group == blocks else terms


def weight_terms(where, video, gain, mine, others, turned_blocks, cots, rows, width, scale, group=2):
    blocks, pixels = len(cots), cots[0].shape[0]
    chans = turned_blocks[0].shape[0] // 2
    outs = cots[0].shape[1]
    whole = pl.BlockSpec(memory_space=pltpu.VMEM)
    smem = pl.BlockSpec(memory_space=pltpu.SMEM)
    taps = LAGS * SIDE * SIDE
    frames = pixels // (rows * width)
    result, input_grad = pl.pallas_call(
        functools.partial(weight_body, blocks, group, rows, width, where.shape[0] - PLACES, scale),
        out_shape=[
            jax.ShapeDtypeStruct((LAGS, SIDE, SIDE, chans, outs), jnp.float32),
            jax.ShapeDtypeStruct(video.shape, video.dtype),
        ],
        in_specs=[smem] + [whole] * (3 + 2 * blocks + len(others)),
        out_specs=[whole, whole],
        scratch_shapes=[pltpu.VMEM((blocks * frames, SIDE * chans, rows * width), turned_blocks[0].dtype)],
        compiler_params=pltpu.CompilerParams(vmem_limit_bytes=8 << 20),
        cost_estimate=pl.CostEstimate(
            flops=2 * blocks * pixels * taps * chans * outs, transcendentals=0, bytes_accessed=8 << 20),
        name="weight_terms",
    )(where, video, gain.reshape(1, -1), mine, *turned_blocks, *cots, *others)
    return result.reshape(taps, chans, outs), input_grad


def extended_2(cells, sides, width):
    for axis, dim in sides:
        count = lax.axis_size(axis)
        ends = count - 1
        head = lax.slice_in_dim(cells, 0, width, axis=dim)
        tail = lax.slice_in_dim(cells, cells.shape[dim] - width, cells.shape[dim], axis=dim)
        cells = jnp.concatenate(
            [
                lax.ppermute(tail, axis, [(i, (i + 1) % count) for i in range(ends)]),
                cells,
                lax.ppermute(head, axis, [((i + 1) % count, i) for i in range(ends)]),
            ],
            axis=dim,
        )
    return cells


def shifted(value, axis, steps):
    count = lax.axis_size(axis)
    leading, last = (max(0, -steps), min(count, count - steps))
    return lax.ppermute(value, axis, [(source, source + steps) for source in range(leading, last)])


def clip_tables(lengths, frame_ids):
    clip_ends = jnp.cumsum(lengths)
    clip_starts = clip_ends - lengths
    clip_ids = jnp.sum((frame_ids[:, None] >= clip_ends[None, :]).astype(jnp.int32), axis=1)
    clip_first = jnp.max(
        jnp.where(clip_starts[None, :] <= frame_ids[:, None], clip_starts[None, :], 0), axis=1
    )
    opening = jnp.any(clip_starts[None, :] == frame_ids[:, None], axis=1)
    return (clip_ids, clip_first, opening)


def input_terms(grad_frames, weights, row_count, col_count):
    frame_total = grad_frames.shape[0]
    local_chans = grad_frames.shape[3]
    all_chans = weights.shape[1]
    pieces = []
    for lag_step in range(3):
        back_stack = jnp.stack(
            [
                grad_frames[
                    :,
                    2 - row_step : 2 - row_step + row_count,
                    2 - col_step : 2 - col_step + col_count,
                    :,
                ]
                for row_step in range(3)
                for col_step in range(3)
            ],
            axis=3,
        ).reshape(frame_total * row_count * col_count, 9 * local_chans)
        back_kernel = jnp.transpose(weights[9 * lag_step : 9 * lag_step + 9], (0, 2, 1)).reshape(
            9 * local_chans, all_chans
        )
        pieces.append(
            jnp.dot(back_stack, back_kernel, preferred_element_type=jnp.float32).reshape(
                frame_total, row_count, col_count, all_chans
            )
        )
    return pieces


def lag_mix(lagged, clip_ids, opening, frame_count):
    here_ids = clip_ids[:frame_count]
    start_flag = opening[:frame_count].astype(jnp.float32)
    act_grad = jnp.zeros((frame_count,) + lagged[0].shape[1:], jnp.float32)
    for lag_step in range(3):
        same_clip = (clip_ids[lag_step : lag_step + frame_count] == here_ids).astype(jnp.float32)
        act_grad = (
            act_grad
            + same_clip[:, None, None, None] * lagged[lag_step][lag_step : lag_step + frame_count]
        )
        for inner_step in range(lag_step):
            near_clip = (clip_ids[inner_step : inner_step + frame_count] == here_ids).astype(
                jnp.float32
            ) * start_flag
            act_grad = (
                act_grad
                + near_clip[:, None, None, None]
                * lagged[lag_step][inner_step : inner_step + frame_count]
            )
    return act_grad


def split_rows(video, channel_gain, weights, lengths, cotangent):
    frame_count, row_count, col_count, local_chans = video.shape
    all_chans = weights.shape[1]
    pixel_count = frame_count * row_count * col_count
    total_pixels = pixel_count * lax.axis_size("tm") * lax.axis_size("rows")
    frame_base = lax.axis_index("tm") * frame_count
    frame_ids = frame_base + jnp.arange(frame_count + 2, dtype=jnp.int32)
    clip_ids, clip_first, opening = clip_tables(lengths, frame_ids)
    own_frames = frame_ids[:frame_count]
    scaled = video.astype(jnp.float32) * channel_gain
    activated = jax.nn.silu(scaled).astype(jnp.bfloat16)
    paired = extended_2(jnp.stack([activated, cotangent]), (("rows", 2),), 1)
    paired = jnp.pad(paired, ((0, 0), (0, 0), (0, 0), (1, 1), (0, 0)))
    act_pad = paired[0]
    grad_pad = paired[1]
    prior_rows = shifted(act_pad, "tm", 1)
    extended = jnp.concatenate([prior_rows, act_pad], axis=0)
    gathered = lax.all_gather(extended, "chan", axis=3, tiled=True)
    flat_grad = cotangent.reshape(pixel_count, local_chans)
    output_sum = jnp.zeros((pixel_count, local_chans), jnp.float32)
    weight_terms = []
    for lag_step in range(3):
        distance = jnp.minimum(lag_step, own_frames - clip_first[:frame_count])[:, None, None, None]
        chosen = jnp.where(
            distance == 0,
            gathered[2 : frame_count + 2],
            jnp.where(distance == 1, gathered[1 : frame_count + 1], gathered[0:frame_count]),
        )
        tap_stack = jnp.stack(
            [
                chosen[:, row_step : row_step + row_count, col_step : col_step + col_count, :]
                for row_step in range(3)
                for col_step in range(3)
            ],
            axis=3,
        ).reshape(pixel_count, 9 * all_chans)
        kernel = weights[9 * lag_step : 9 * lag_step + 9].reshape(9 * all_chans, local_chans)
        output_sum = output_sum + jnp.dot(tap_stack, kernel, preferred_element_type=jnp.float32)
        weight_terms.append(
            lax.dot_general(
                tap_stack, flat_grad, (((0,), (0,)), ((), ())), preferred_element_type=jnp.float32
            ).reshape(9, all_chans, local_chans)
        )
    output = (
        video.astype(jnp.float32)
        + output_sum.reshape(frame_count, row_count, col_count, local_chans)
    ).astype(jnp.bfloat16)
    own_terms = lax.psum_scatter(
        jnp.stack(input_terms(grad_pad, weights, row_count, col_count)),
        "chan",
        scatter_dimension=4,
        tiled=True,
    )
    arriving = shifted(
        jnp.concatenate([own_terms[1, 0:1], own_terms[2, 0:2]], axis=0).astype(jnp.bfloat16),
        "tm",
        -1,
    ).astype(jnp.float32)
    lagged = [
        own_terms[0],
        jnp.concatenate([own_terms[1], arriving[0:1]], axis=0),
        jnp.concatenate([own_terms[2], arriving[1:3]], axis=0),
    ]
    act_grad = lag_mix(lagged, clip_ids, opening, frame_count)
    sigmoid_value = jax.nn.sigmoid(scaled)
    slope_factor = sigmoid_value * (1.0 + scaled * (1.0 - sigmoid_value))
    input_grad = (cotangent.astype(jnp.float32) + act_grad * slope_factor * channel_gain).astype(
        jnp.bfloat16
    )
    weight_sum = jnp.concatenate(weight_terms, axis=0)
    summed = lax.psum_scatter(weight_sum, ("tm", "rows"), scatter_dimension=1, tiled=True)
    weight_grad = summed * (1.0 / math.sqrt(total_pixels))
    return (output, input_grad, weight_grad)


def along(value, axis, steps):
    count = lax.axis_size(axis)
    first, last = max(0, -steps), min(count, count - steps)
    return lax.ppermute(value, axis, [(source, source + steps) for source in range(first, last)])


def across(value, axis, offset):
    return lax.ppermute(value, axis, [(i, i ^ offset) for i in range(lax.axis_size(axis))])


def ahead(value, axis, steps):
    count = lax.axis_size(axis)
    return lax.ppermute(value, axis, [((i + steps) % count, i) for i in range(count)])


def gathered_blocks(own, axis):
    blocks = {0: own}
    bit = lax.axis_size(axis) // 2
    while bit:
        for offset in list(blocks):
            blocks[offset ^ bit] = across(blocks[offset], axis, bit)
        bit //= 2
    return [blocks[offset] for offset in range(len(blocks))]


def whole_rows(video, channel_gain, weights, lengths, cotangent):
    frames, rows, width, chans = video.shape
    all_chans = weights.shape[1]
    parts, shards = all_chans // chans, lax.axis_size("tm")
    pixels = frames * rows * width
    weights = pltpu.with_memory_space_constraint(weights, pltpu.HBM)
    weights = pltpu.with_memory_space_constraint(weights, pltpu.VMEM)
    shard, chan = lax.axis_index("tm"), lax.axis_index("chan")
    where = jnp.concatenate([jnp.stack([shard * frames, chan, shard]), lengths]).astype(jnp.int32)
    activated = silu(video.reshape(pixels, chans), channel_gain).reshape(video.shape)
    own = [activated] + [ahead(activated, "chan", j) for j in range(1, parts)]
    before = along(activated, "tm", 1)
    past = [before] + [ahead(before, "chan", j) for j in range(1, parts)]
    later = along(cotangent, "tm", -1)
    cots = gathered_blocks(cotangent.reshape(pixels, chans), "tm")
    mine, *others = backward(where, cotangent, later, weights)
    others = [ahead(others[j - 1], "chan", parts - j).reshape(pixels, chans) for j in range(1, parts)]
    sent = turned(where, [x.reshape(pixels, chans) for x in own], shards // 2)
    blocks = []
    for offset in range(shards // 2):
        block = across(sent[offset], "tm", 2 * offset) if offset else sent[0]
        blocks += [block, across(block, "tm", 1)]
    output = forward(where, video, own, past, weights)
    scale = 1.0 / math.sqrt(pixels * shards)
    weight_grad, input_grad = weight_terms(
        where, video.reshape(pixels, chans), channel_gain, mine.reshape(pixels, chans), others, blocks, cots,
        rows, width, scale,
    )
    return (output, input_grad.reshape(video.shape), weight_grad)


def solution(mesh):
    in_specs = (
        P(("groups", "tm"), "rows", None, "chan"),
        P("chan"),
        P(None, None, "chan"),
        P("groups"),
        P(("groups", "tm"), "rows", None, "chan"),
    )
    out_specs = (
        P(("groups", "tm"), "rows", None, "chan"),
        P(("groups", "tm"), "rows", None, "chan"),
        P("groups", ("tm", "rows"), "chan"),
    )
    body = whole_rows if mesh.shape["rows"] == 1 else split_rows
    return jax.shard_map(body, mesh=mesh, in_specs=in_specs, out_specs=out_specs, check_vma=False)
```
